32 devices in a mesh: dp: 16 (over z, x, core), mlp: 2 (over y).
Axes of the slice: x: 2, y: 2, z: 4, core: 2. Of those that a mesh axis runs over, the one named last changes fastest.
Arguments:
- patches: bfloat16 [24576, 768], P(('dp', 'mlp')), may hold values from -6 to 6
- image_of_patch: int32 [16, 1536], P('dp'), may hold values from 0 to 3, never falling along the last dimension, each value on 1 to 576 neighbouring positions
- patch_row: int32 [16, 1536], P('dp'), may hold values from 0 to 23
- patch_col: int32 [16, 1536], P('dp'), may hold values from 0 to 23
- ln1_gain: float32 [768], replicated, may hold values from 0.1 to 1.9
- ln1_bias: float32 [768], replicated, may hold values from -1.75 to 1.75
- w_qkv: bfloat16 [768, 2304], replicated, may hold values from -0.21875 to 0.21875
- b_qkv: float32 [2304], replicated, may hold values from -1.75 to 1.75
- freqs: float32 [2, 384], replicated, may hold values from -0.5 to 0.5
- w_out: bfloat16 [768, 768], replicated, may hold values from -1.75 to 1.75
- b_out: float32 [768], replicated, may hold values from -1.75 to 1.75
- ln2_gain: float32 [768], replicated, may hold values from 0.1 to 1.9
- ln2_bias: float32 [768], replicated, may hold values from -1.75 to 1.75
- w_up: bfloat16 [768, 3072], P(None, 'mlp'), may hold values from -0.21875 to 0.21875
- b_up: float32 [3072], P('mlp'), may hold values from -1.75 to 1.75
- w_down: bfloat16 [3072, 768], P('mlp'), may hold values from -0.109375 to 0.109375
- b_down: float32 [768], replicated, may hold values from -1.75 to 1.75
- out_cotangent: bfloat16 [24576, 768], P(('dp', 'mlp')), may hold values from -6 to 6
Outputs:
- block_out: bfloat16 [24576, 768], P(('dp', 'mlp'))
- grad_patches: bfloat16 [24576, 768], P(('dp', 'mlp'))
- grad_ln1_gain: float32 [768], replicated
- grad_ln1_bias: float32 [768], replicated
- grad_w_qkv: float32 [768, 2304], replicated
- grad_b_qkv: float32 [2304], replicated
- grad_freqs: float32 [2, 384], replicated
- grad_w_out: float32 [768, 768], replicated
- grad_b_out: float32 [768], replicated
- grad_ln2_gain: float32 [768], replicated
- grad_ln2_bias: float32 [768], replicated
- grad_w_up: float32 [768, 3072], P(None, 'mlp')
- grad_b_up: float32 [3072], P('mlp')
- grad_w_down: float32 [3072, 768], P('mlp')
- grad_b_down: float32 [768], replicated
The draws below stay inside these ranges and needn't reach their ends.
Inputs may be any that keep to these rules, and one draw needn't show every extreme that they name: `image_of_patch`: within each group the image numbers never fall, every image has 1 to 576 patches, and some image has exactly 576.
All inputs are finite; a program needn't handle non-finite values.
Results may differ from the reference program's by a relative error of at most 0.013.
Values may be sent and summed in bfloat16 or wider, within the bound.
A program may use at most 192 MiB of HBM per device.

```python
import math
import jax
import jax.numpy as jnp
import numpy as np
from jax import lax

D = 768
H = 12
HD = 64
FF = 3072
SEQ = 1536
GROUPS = 16
TOKENS = 24576
IMG_MOST = 576
COUNT = 4


def touch_ends(values, rng, least, largest):
    index_at = [jax.random.randint(jax.random.fold_in(rng, axis), (), 0, length) for axis, length in enumerate(values.shape)]
    widest = values.shape.index(max(values.shape))
    next_to = index_at[:widest] + [(index_at[widest] + 1) % values.shape[widest]] + index_at[widest + 1:]
    return values.at[tuple(index_at)].set(least).at[tuple(next_to)].set(largest)


def block_levels(rng, dims, split, low, top_value):
    def one(position, blocks):
        steps = jax.random.uniform(jax.random.fold_in(jax.random.fold_in(rng, 6), position), (blocks,), jnp.float32, low / len(split), top_value / len(split))
        return jnp.repeat(jnp.exp(steps), dims[position] // blocks).reshape((-1,) + (1,) * (len(dims) - position - 1))

    factor_of = one(*split[0])
    for cut in split[1:]:
        factor_of = factor_of * one(*cut)
    return factor_of


def length_profile(count, total, bound, skew):
    loads = [(1 << 20) // math.isqrt(standing ** skew) + 1 for standing in range(2, count + 1)]
    spare, holding = total - bound - (count - 1), [1] * (count - 1)
    while spare > 0:
        movable = [i for i in range(count - 1) if holding[i] < bound]
        pool, remaining = sum([loads[i] for i in movable]), spare
        for i in movable:
            more = min(bound - holding[i], max(1, remaining * loads[i] // pool), spare)
            holding[i] = holding[i] + more
            spare = spare - more
    return np.array([bound] + holding)


def ragged_sizes(key, number_of, total, bound, slope):
    if number_of == 2:
        one = jax.random.randint(key, (), max(1, total - bound), min(bound, total - 1) + 1)
        return jnp.stack([one, total - one])
    sizes = jnp.asarray(length_profile(number_of, total, bound, slope), jnp.int32)
    twos = (number_of - 1) // 2
    donor, taker = sizes[1:1 + 2 * twos:2], sizes[2:2 + 2 * twos:2]
    room = jnp.minimum(donor - 1, bound - taker)
    shifted = jax.random.randint(jax.random.fold_in(key, 1), (twos,), 0, 1 << 20) % (room + 1)
    sizes = sizes.at[1:1 + 2 * twos:2].set(donor - shifted).at[2:2 + 2 * twos:2].set(taker + shifted)
    return sizes[jax.random.permutation(jax.random.fold_in(key, 2), number_of)]


def normal_values(key, shape, scale, bound, pieces=(), dtype=jnp.bfloat16):
    drawn = jax.random.normal(key, shape, jnp.float32) * scale
    if len(pieces) > 0:
        drawn = block_levels(key, shape, pieces, -0.22, 0.18) * drawn
    return jnp.clip(drawn, min=-bound, max=bound).astype(dtype)


def setup_inputs(seed: int = 0) -> dict:
    streams_of = jax.random.split(jax.random.key(seed), 19)
    patches = normal_values(streams_of[0], (TOKENS, D), 1.0, 6.0, ((0, 32),))
    image_of_patch = jax.vmap(lambda own: jnp.searchsorted(jnp.cumsum(ragged_sizes(own, COUNT, SEQ, IMG_MOST, 1)), jnp.arange(SEQ), side="right"))(jax.random.split(streams_of[1], GROUPS)).reshape((GROUPS, SEQ)).astype(jnp.int32)
    patch_row = touch_ends(jax.random.randint(streams_of[2], (GROUPS, SEQ), 0, 24), jax.random.fold_in(streams_of[2], 1), 0, 23).astype(jnp.int32)
    patch_col = touch_ends(jax.random.randint(streams_of[3], (GROUPS, SEQ), 0, 24), jax.random.fold_in(streams_of[3], 1), 0, 23).astype(jnp.int32)
    ln1_gain = jnp.clip(1.0 + 0.18 * jax.random.normal(streams_of[4], (D,), jnp.float32), 0.1, 1.9)
    ln1_bias = normal_values(streams_of[5], (D,), 0.3, 1.75, (), jnp.float32)
    w_qkv = normal_values(streams_of[6], (D, 3 * D), D ** -0.5, 0.21875)
    b_qkv = normal_values(streams_of[7], (3 * D,), 0.3, 1.75, (), jnp.float32)
    freqs = jnp.clip(jax.random.uniform(streams_of[8], (2, D // 2), jnp.float32, -0.5, 0.5), -0.5, 0.5)
    w_out = normal_values(streams_of[9], (D, D), (D // 64) ** -0.5, 1.75)
    b_out = normal_values(streams_of[10], (D,), 0.3, 1.75, (), jnp.float32)
    ln2_gain = jnp.clip(1.0 + 0.18 * jax.random.normal(streams_of[11], (D,), jnp.float32), 0.1, 1.9)
    ln2_bias = normal_values(streams_of[12], (D,), 0.3, 1.75, (), jnp.float32)
    w_up = normal_values(streams_of[13], (D, FF), D ** -0.5, 0.21875, ((1, 2),))
    b_up = normal_values(streams_of[14], (FF,), 0.3, 1.75, ((0, 2),), jnp.float32)
    w_down = normal_values(streams_of[15], (FF, D), FF ** -0.5, 0.109375, ((0, 2),))
    b_down = normal_values(streams_of[16], (D,), 0.3, 1.75, (), jnp.float32)
    out_cotangent = normal_values(streams_of[17], (TOKENS, D), 1.0, 6.0, ((0, 32),))
    return dict(patches=patches, image_of_patch=image_of_patch, patch_row=patch_row, patch_col=patch_col, ln1_gain=ln1_gain, ln1_bias=ln1_bias, w_qkv=w_qkv, b_qkv=b_qkv, freqs=freqs, w_out=w_out, b_out=b_out, ln2_gain=ln2_gain, ln2_bias=ln2_bias, w_up=w_up, b_up=b_up, w_down=w_down, b_down=b_down, out_cotangent=out_cotangent)


EPSILON = 1e-06
HIGHEST = lax.Precision.HIGHEST

@jax.custom_vjp
def low(v):
    return lax.optimization_barrier(v.astype(jnp.bfloat16)).astype(jnp.float32)

@jax.custom_vjp
def low_back(v):
    return v

def low_keep(v):
    return (low(v), None)

def low_pass(kept, grad):
    return (grad,)

def back_keep(v):
    return (v, None)

def back_low(kept, grad):
    return (low(grad),)
low.defvjp(low_keep, low_pass)
low_back.defvjp(back_keep, back_low)

def layer_norm(values, gain, shift):
    center = values - lax.optimization_barrier(jnp.mean(values, axis=-1, keepdims=True))
    spread = lax.optimization_barrier(jnp.mean(center * center, axis=-1, keepdims=True))
    return center * lax.rsqrt(spread + EPSILON) * gain + shift

def angles(row_pos, col_pos, freq_table):
    freq_row = freq_table[0].reshape(H, HD // 2)
    freq_col = freq_table[1].reshape(H, HD // 2)
    return row_pos[:, None, None] * freq_row[None] + col_pos[:, None, None] * freq_col[None]

def rotate(values, angle):
    half = values.shape[-1] // 2
    first = values[..., :half]
    second = values[..., half:]
    cosine = jnp.cos(angle)
    sine = jnp.sin(angle)
    return jnp.concatenate([first * cosine - second * sine, first * sine + second * cosine], axis=-1)

def group_forward(inputs, image_ids, row_pos, col_pos, params):
    ln1_gain, ln1_bias, w_qkv, b_qkv, freqs, w_out, b_out, ln2_gain, ln2_bias, w_up, b_up, w_down, b_down = params
    length = inputs.shape[0]
    normed = low(layer_norm(inputs, ln1_gain, ln1_bias))
    qkv = low_back(jnp.dot(normed, w_qkv, precision=HIGHEST) + b_qkv)
    angle = angles(row_pos, col_pos, freqs)
    query = low(rotate(qkv[:, :D].reshape(length, H, HD), angle))
    keys = low(rotate(qkv[:, D:2 * D].reshape(length, H, HD), angle))
    values = low(qkv[:, 2 * D:].reshape(length, H, HD))
    raw = low_back(jnp.einsum('qhd,khd->hqk', query, keys, precision=HIGHEST) * HD ** (-0.5))
    same_image = image_ids[:, None] == image_ids[None, :]
    scores = jnp.where(same_image[None], raw, -1e+30)
    prob = jax.nn.softmax(scores, axis=-1)
    mixed = jnp.einsum('hqk,khd->qhd', low(prob), values, precision=HIGHEST)
    mixed = low(low_back(mixed)).reshape(length, D)
    attended = low_back(jnp.dot(mixed, w_out, precision=HIGHEST) + b_out)
    middle = inputs + attended
    normed2 = low(layer_norm(middle, ln2_gain, ln2_bias))
    pre = low_back(jnp.dot(normed2, w_up, precision=HIGHEST) + b_up)
    hidden = low(jax.nn.gelu(pre, approximate=False))
    return middle + jnp.dot(hidden, w_down, precision=HIGHEST) + b_down

def reference(patches, image_of_patch, patch_row, patch_col, ln1_gain, ln1_bias, w_qkv, b_qkv, freqs, w_out, b_out, ln2_gain, ln2_bias, w_up, b_up, w_down, b_down, out_cotangent):
    params = (ln1_gain, ln1_bias, w_qkv.astype(jnp.float32), b_qkv, freqs, w_out.astype(jnp.float32), b_out, ln2_gain, ln2_bias, w_up.astype(jnp.float32), b_up, w_down.astype(jnp.float32), b_down)
    inputs = patches.astype(jnp.float32).reshape(GROUPS, SEQ, D)
    cotangent = out_cotangent.astype(jnp.float32).reshape(GROUPS, SEQ, D)
    row_float = patch_row.astype(jnp.float32)
    col_float = patch_col.astype(jnp.float32)
    zeros = jax.tree.map(jnp.zeros_like, params)

    def group_step(totals, item):
        group_in, group_cot, group_ids, group_rows, group_cols = item

        def forward(values, weights):
            return group_forward(values, group_ids, group_rows, group_cols, weights)
        result, backward = jax.vjp(jax.checkpoint(forward), group_in, params)
        grad_in, grad_params = backward(group_cot)
        totals = jax.tree.map(jnp.add, totals, grad_params)
        return (totals, (result, grad_in))
    totals, (outputs, grad_inputs) = lax.scan(group_step, zeros, (inputs, cotangent, image_of_patch, row_float, col_float))
    block_out = outputs.reshape(TOKENS, D).astype(jnp.bfloat16)
    grad_patches = grad_inputs.reshape(TOKENS, D).astype(jnp.bfloat16)
    return (block_out, grad_patches, totals[0], totals[1], totals[2], totals[3], totals[4], totals[5], totals[6], totals[7], totals[8], totals[9], totals[10], totals[11], totals[12])
```

```python
from functools import partial

import jax
import jax.numpy as jnp
from jax import lax
from jax.experimental import pallas as pl
from jax.experimental.pallas import tpu as pltpu
from jax.sharding import PartitionSpec as P

H = 12
HD = 64
PAIRS = H // 2
LANES = 128
EPSILON = 1e-06
MOST = 576
SIDE = 24
KEY_TILE = 128
QUERY_TILE = 256
EDGE = -(-(MOST - 1) // KEY_TILE) * KEY_TILE
VMEM_LIMIT = 60 * 1024 * 1024
BF = jnp.bfloat16
F32 = jnp.float32


def dot(left, right):
    return jnp.dot(left, right, preferred_element_type=F32)


def dot_nt(left, right):
    return lax.dot_general(left, right, (((1,), (1,)), ((), ())), preferred_element_type=F32)


def dot_tn(left, right):
    return lax.dot_general(left, right, (((0,), (0,)), ((), ())), preferred_element_type=F32)


def split3(values):
    high = lax.reduce_precision(values, 8, 7)
    rest = values - high
    mid = lax.reduce_precision(rest, 8, 7)
    low = rest - mid
    return jnp.concatenate([high, mid, low], axis=0).astype(BF)


def rope_table(freqs):
    wide = jnp.concatenate([freqs.reshape(2, H, 1, HD // 2)] * 2, axis=2).reshape(2, H * HD)
    steps = jnp.arange(SIDE, dtype=F32)[:, None]
    row_angle = steps * wide[0][None]
    col_angle = steps * wide[1][None]
    row_part = jnp.concatenate([split3(jnp.cos(row_angle)), split3(jnp.sin(row_angle))], axis=1)
    col_part = jnp.concatenate([split3(jnp.cos(col_angle)), split3(jnp.sin(col_angle))], axis=1)
    zero = jnp.zeros_like(row_part)
    table = jnp.concatenate(
        [jnp.concatenate([row_part, zero], axis=1), jnp.concatenate([zero, col_part], axis=1)],
        axis=0,
    )
    return jnp.pad(table, ((0, 256 - table.shape[0]), (0, 0)))


def cos_sin(row_pos, col_pos, table, first, width):
    rows = row_pos.shape[0]
    full = H * HD
    lane = lax.broadcasted_iota(jnp.int32, (rows, 256), 1)
    part = lane % SIDE
    part = jnp.where(lane < 6 * SIDE, part, -1)
    hot = jnp.where(jnp.where(lane < 3 * SIDE, row_pos, col_pos) == part, 1.0, 0.0).astype(BF)
    parts = [dot(hot, table[:, k * full + first : k * full + first + width]) for k in range(4)]
    cos_r, sin_r, cos_c, sin_c = parts
    cosine = cos_r * cos_c - sin_r * sin_c
    sine = sin_r * cos_c + cos_r * sin_c
    lane_out = lax.broadcasted_iota(jnp.int32, (rows, width), 1)
    signed = jnp.where(lane_out % HD < HD // 2, -sine, sine)
    return cosine, signed


def swap_halves(slab):
    lane = lax.broadcasted_iota(jnp.int32, slab.shape, 1)
    return jnp.where(
        lane % HD < HD // 2,
        pltpu.roll(slab, LANES - HD // 2, 1),
        pltpu.roll(slab, HD // 2, 1),
    )


def input_kernel(with_query, x_ref, row_ref, col_ref, gain_ref, bias_ref, w_ref, b_ref, t_ref, *outs):
    width = x_ref.shape[1]
    if with_query:
        normed_ref, q_ref, k_ref, v_ref = outs
    else:
        normed_ref, k_ref, v_ref = outs
        q_ref = None
    values = x_ref[...].astype(F32)
    center = values - jnp.mean(values, axis=-1, keepdims=True)
    spread = jnp.mean(center * center, axis=-1, keepdims=True)
    normed = (center * lax.rsqrt(spread + EPSILON) * gain_ref[...] + bias_ref[...]).astype(BF)
    normed_ref[...] = normed
    row_pos = row_ref[...]
    col_pos = col_ref[...]
    for pair in range(PAIRS):
        cut = slice(pair * LANES, (pair + 1) * LANES)
        cosine, sine = cos_sin(row_pos, col_pos, t_ref, pair * LANES, LANES)
        for kind, out_ref in ((0, q_ref), (1, k_ref)):
            if out_ref is None:
                continue
            here = slice(kind * width + pair * LANES, kind * width + (pair + 1) * LANES)
            pre = dot(normed, w_ref[:, here]) + b_ref[:, here]
            out_ref[:, cut] = (pre * cosine + swap_halves(pre) * sine).astype(BF)
    v_ref[...] = (dot(normed, w_ref[:, 2 * width :]) + b_ref[:, 2 * width :]).astype(BF)


def input_stage(x, row_col, col_col, gain, bias, w_qkv, b_qkv, table, with_query, tile):
    rows, width = x.shape
    tiled = lambda cols: pl.BlockSpec((tile, cols), lambda i: (i, 0))
    whole = lambda a: pl.BlockSpec(a.shape, lambda i: (0, 0))
    outs = 4 if with_query else 3
    return pl.pallas_call(
        partial(input_kernel, with_query),
        grid=(rows // tile,),
        in_specs=[tiled(width), tiled(1), tiled(1)] + [whole(a) for a in (gain, bias, w_qkv, b_qkv, table)],
        out_specs=[tiled(width)] * outs,
        out_shape=[jax.ShapeDtypeStruct((rows, width), BF)] * outs,
        compiler_params=pltpu.CompilerParams(vmem_limit_bytes=VMEM_LIMIT),
        cost_estimate=pl.CostEstimate(
            flops=2 * rows * width * width * (4 if with_query else 3),
            bytes_accessed=int(w_qkv.size * 2 + rows * width * 2 * 5),
            transcendentals=0,
        ),
        name="ln_qkv_rope",
    )(x, row_col, col_col, gain, bias, w_qkv, b_qkv, table)


def head_lanes(shape, side):
    lane = lax.broadcasted_iota(jnp.int32, shape, 1)
    return (lane < HD) if side == 0 else (lane >= HD)


def visible(ids_ref, query_tile, key_tile):
    q0 = query_tile * QUERY_TILE
    k0 = key_tile * KEY_TILE
    return (ids_ref[0, k0] <= ids_ref[0, q0 + QUERY_TILE - 1]) & (
        ids_ref[0, k0 + KEY_TILE - 1] >= ids_ref[0, q0]
    )


def attend_kernel(ids_ref, q_ref, k_own_ref, k_edge_ref, v_own_ref, v_edge_ref, idk_ref, idq_ref,
                  mixed_ref, out_t_ref, lse_ref, key_sc, value_t_sc, peak_sc, total_sc, acc_sc):
    own = k_own_ref.shape[0]
    rows = key_sc.shape[0]
    step = pl.program_id(0)

    @pl.when(step == 0)
    def _():
        key_sc[0:own, :] = k_own_ref[...]
        key_sc[own:rows, :] = k_edge_ref[...]
        for start in range(0, rows, KEY_TILE):
            for pair in range(PAIRS):
                cut = slice(pair * LANES, (pair + 1) * LANES)
                if start < own:
                    block = v_own_ref[start : start + KEY_TILE, cut]
                else:
                    block = v_edge_ref[start - own : start - own + KEY_TILE, cut]
                value_t_sc[start // KEY_TILE, cut, :] = jnp.transpose(block.astype(F32)).astype(BF)

    peak_sc[...] = jnp.full(peak_sc.shape, -1e30, F32)
    total_sc[...] = jnp.zeros(total_sc.shape, F32)
    acc_sc[...] = jnp.zeros(acc_sc.shape, F32)
    scale = HD ** (-0.5)

    @pl.loop(0, rows // KEY_TILE)
    def _(tile):
        @pl.when(visible(ids_ref, step, tile))
        def _():
            k0 = pl.multiple_of(tile * KEY_TILE, KEY_TILE)
            allowed = idk_ref[pl.ds(k0, KEY_TILE), :] == idq_ref[...]
            for head in range(H):
                pair, side = head // 2, head % 2
                cut = slice(pair * LANES, (pair + 1) * LANES)
                query = q_ref[:, cut]
                query = jnp.where(head_lanes(query.shape, side), query * BF(scale), BF(0))
                scores = dot_nt(key_sc[pl.ds(k0, KEY_TILE), cut], query)
                scores = jnp.where(allowed, scores, -1e30)
                before = peak_sc[head : head + 1, :]
                peak = jnp.maximum(before, jnp.max(scores, axis=0, keepdims=True))
                expo = jnp.exp(scores - peak)
                fade = jnp.exp(before - peak)
                peak_sc[head : head + 1, :] = peak
                total_sc[head : head + 1, :] = fade * total_sc[head : head + 1, :] + jnp.sum(
                    expo, axis=0, keepdims=True
                )
                part = slice(head * HD, (head + 1) * HD)
                acc_sc[part, :] = fade * acc_sc[part, :] + dot(value_t_sc[tile, part, :], expo.astype(BF))

    lse_ref[...] = peak_sc[...] + jnp.log(jnp.maximum(total_sc[...], 1e-30))
    for head in range(H):
        part = slice(head * HD, (head + 1) * HD)
        acc_sc[part, :] = acc_sc[part, :] / total_sc[head : head + 1, :]
    out_t_ref[...] = acc_sc[...]
    for pair in range(PAIRS):
        cut = slice(pair * LANES, (pair + 1) * LANES)
        mixed_ref[:, cut] = jnp.transpose(acc_sc[cut, :]).astype(BF)


def attend(ids, q, k_own, k_edge, v_own, v_edge, id_col, id_row):
    own, width = q.shape
    rows = own + k_edge.shape[0]
    whole = lambda a: pl.BlockSpec(a.shape, lambda i: (0, 0))
    return pl.pallas_call(
        attend_kernel,
        grid=(own // QUERY_TILE,),
        in_specs=[
            pl.BlockSpec(memory_space=pltpu.SMEM),
            pl.BlockSpec((QUERY_TILE, width), lambda i: (i, 0)),
            whole(k_own), whole(k_edge), whole(v_own), whole(v_edge), whole(id_col),
            pl.BlockSpec((1, QUERY_TILE), lambda i: (0, i)),
        ],
        out_specs=[
            pl.BlockSpec((QUERY_TILE, width), lambda i: (i, 0)),
            pl.BlockSpec((width, QUERY_TILE), lambda i: (0, i)),
            pl.BlockSpec((16, QUERY_TILE), lambda i: (0, i)),
        ],
        out_shape=[
            jax.ShapeDtypeStruct((own, width), BF),
            jax.ShapeDtypeStruct((width, own), F32),
            jax.ShapeDtypeStruct((16, own), F32),
        ],
        scratch_shapes=[
            pltpu.VMEM((rows, width), BF),
            pltpu.VMEM((rows // KEY_TILE, width, KEY_TILE), BF),
            pltpu.VMEM((16, QUERY_TILE), F32),
            pltpu.VMEM((16, QUERY_TILE), F32),
            pltpu.VMEM((width, QUERY_TILE), F32),
        ],
        compiler_params=pltpu.CompilerParams(vmem_limit_bytes=VMEM_LIMIT),
        cost_estimate=pl.CostEstimate(
            flops=4 * own * rows * width, bytes_accessed=int(rows * width * 8), transcendentals=own * rows * H // 2
        ),
        name="attend",
    )(ids, q, k_own, k_edge, v_own, v_edge, id_col, id_row)


def unrotate(grad, rotated, row_pos, col_pos, table, first):
    cosine, sine = cos_sin(row_pos, col_pos, table, first, LANES)
    lane = lax.broadcasted_iota(jnp.int32, grad.shape, 1)
    turned = swap_halves(rotated)
    angle = grad * jnp.where(lane % HD < HD // 2, -turned, turned)
    return grad * cosine - swap_halves(grad) * sine, angle


def attend_back_kernel(ids_ref, q_ref, g_ref, k_own_ref, k_edge_ref, v_own_ref, v_edge_ref, idk_ref,
                       idq_ref, out_t_ref, lse_ref, row_ref, col_ref, rowq_ref, colq_ref, t_ref,
                       dq_ref, dk_ref, dv_ref, freq_ref, sums_ref,
                       key_sc, value_sc, key_t_sc, dk_sc, dv_sc, dq_t_sc, delta_sc):
    own, width = k_own_ref.shape
    rows = key_sc.shape[0]
    step = pl.program_id(0)
    scale = HD ** (-0.5)

    @pl.when(step == 0)
    def _():
        key_sc[0:own, :] = k_own_ref[...]
        key_sc[own:rows, :] = k_edge_ref[...]
        value_sc[0:own, :] = v_own_ref[...]
        value_sc[own:rows, :] = v_edge_ref[...]
        for start in range(0, rows, KEY_TILE):
            for pair in range(PAIRS):
                cut = slice(pair * LANES, (pair + 1) * LANES)
                if start < own:
                    block = k_own_ref[start : start + KEY_TILE, cut]
                else:
                    block = k_edge_ref[start - own : start - own + KEY_TILE, cut]
                key_t_sc[start // KEY_TILE, cut, :] = jnp.transpose(block.astype(F32)).astype(BF)
        dk_sc[...] = jnp.zeros(dk_sc.shape, F32)
        dv_sc[...] = jnp.zeros(dv_sc.shape, F32)
        freq_ref[...] = jnp.zeros(freq_ref.shape, F32)
        sums_ref[...] = jnp.zeros(sums_ref.shape, F32)

    dq_t_sc[...] = jnp.zeros(dq_t_sc.shape, F32)
    for pair in range(PAIRS):
        cut = slice(pair * LANES, (pair + 1) * LANES)
        grad_t = jnp.transpose(g_ref[:, cut].astype(F32)) * out_t_ref[cut, :]
        for side in range(2):
            delta_sc[2 * pair + side : 2 * pair + side + 1, :] = jnp.sum(
                grad_t[side * HD : (side + 1) * HD, :], axis=0, keepdims=True
            )

    @pl.loop(0, rows // KEY_TILE)
    def _(tile):
        @pl.when(visible(ids_ref, step, tile))
        def _():
            k0 = pl.multiple_of(tile * KEY_TILE, KEY_TILE)
            allowed = idk_ref[pl.ds(k0, KEY_TILE), :] == idq_ref[...]
            for pair in range(PAIRS):
                cut = slice(pair * LANES, (pair + 1) * LANES)
                keys = key_sc[pl.ds(k0, KEY_TILE), cut]
                values = value_sc[pl.ds(k0, KEY_TILE), cut]
                add_k = None
                add_v = None
                for side in range(2):
                    head = 2 * pair + side
                    query = q_ref[:, cut]
                    mine = head_lanes(query.shape, side)
                    query = jnp.where(mine, query * BF(scale), BF(0))
                    grad = jnp.where(mine, g_ref[:, cut], BF(0))
                    scores = dot_nt(keys, query)
                    weights = jnp.where(allowed, jnp.exp(scores - lse_ref[head : head + 1, :]), 0.0)
                    grad_w = dot_nt(values, grad)
                    grad_s = (weights * (grad_w - delta_sc[head : head + 1, :])).astype(BF)
                    one_v = dot(weights.astype(BF), grad)
                    one_k = dot(grad_s, query)
                    add_v = one_v if side == 0 else add_v + one_v
                    add_k = one_k if side == 0 else add_k + one_k
                    part = slice(head * HD, (head + 1) * HD)
                    dq_t_sc[part, :] += dot(key_t_sc[tile, part, :], grad_s)
                dv_sc[pl.ds(k0, KEY_TILE), cut] += add_v
                dk_sc[pl.ds(k0, KEY_TILE), cut] += add_k

    row_f = rowq_ref[...].astype(F32)
    col_f = colq_ref[...].astype(F32)
    for pair in range(PAIRS):
        cut = slice(pair * LANES, (pair + 1) * LANES)
        grad = jnp.transpose(dq_t_sc[cut, :]) * scale
        back, angle = unrotate(grad, q_ref[:, cut].astype(F32), rowq_ref[...], colq_ref[...], t_ref, pair * LANES)
        back = back.astype(BF)
        dq_ref[:, cut] = back
        freq_ref[0:1, cut] += jnp.sum(angle * row_f, axis=0, keepdims=True)
        freq_ref[1:2, cut] += jnp.sum(angle * col_f, axis=0, keepdims=True)
        sums_ref[0:1, cut] += jnp.sum(back.astype(F32), axis=0, keepdims=True)

    @pl.when(step == pl.num_programs(0) - 1)
    def _():
        @pl.loop(0, rows // KEY_TILE)
        def _(tile):
            k0 = pl.multiple_of(tile * KEY_TILE, KEY_TILE)
            here = pl.ds(k0, KEY_TILE)
            row_pos = row_ref[here, :]
            col_pos = col_ref[here, :]
            for pair in range(PAIRS):
                cut = slice(pair * LANES, (pair + 1) * LANES)
                back, angle = unrotate(
                    dk_sc[here, cut], key_sc[here, cut].astype(F32), row_pos, col_pos, t_ref, pair * LANES
                )
                back = back.astype(BF)
                dk_ref[here, cut] = back
                freq_ref[0:1, cut] += jnp.sum(angle * row_pos.astype(F32), axis=0, keepdims=True)
                freq_ref[1:2, cut] += jnp.sum(angle * col_pos.astype(F32), axis=0, keepdims=True)
                sums_ref[1:2, cut] += jnp.sum(back.astype(F32), axis=0, keepdims=True)
                grad_v = dv_sc[here, cut].astype(BF)
                dv_ref[here, cut] = grad_v
                sums_ref[2:3, cut] += jnp.sum(grad_v.astype(F32), axis=0, keepdims=True)


def attend_back(ids, q, grad_mixed, k_own, k_edge, v_own, v_edge, id_col, id_row, out_t, lse, row_col, col_col, table):
    own, width = q.shape
    rows = own + k_edge.shape[0]
    whole = lambda a: pl.BlockSpec(a.shape, lambda i: (0, 0))
    tiled = pl.BlockSpec((QUERY_TILE, width), lambda i: (i, 0))
    across = lambda n: pl.BlockSpec((n, QUERY_TILE), lambda i: (0, i))
    thin = pl.BlockSpec((QUERY_TILE, 1), lambda i: (i, 0))
    full = pl.BlockSpec((rows, width), lambda i: (0, 0))
    small = pl.BlockSpec((8, width), lambda i: (0, 0))
    return pl.pallas_call(
        attend_back_kernel,
        grid=(own // QUERY_TILE,),
        in_specs=[
            pl.BlockSpec(memory_space=pltpu.SMEM), tiled, tiled,
            whole(k_own), whole(k_edge), whole(v_own), whole(v_edge), whole(id_col),
            across(1), across(width), across(16), whole(row_col), whole(col_col), thin, thin, whole(table),
        ],
        out_specs=[tiled, full, full, small, small],
        out_shape=[
            jax.ShapeDtypeStruct((own, width), BF),
            jax.ShapeDtypeStruct((rows, width), BF),
            jax.ShapeDtypeStruct((rows, width), BF),
            jax.ShapeDtypeStruct((8, width), F32),
            jax.ShapeDtypeStruct((8, width), F32),
        ],
        scratch_shapes=[
            pltpu.VMEM((rows, width), BF),
            pltpu.VMEM((rows, width), BF),
            pltpu.VMEM((rows // KEY_TILE, width, KEY_TILE), BF),
            pltpu.VMEM((rows, width), F32),
            pltpu.VMEM((rows, width), F32),
            pltpu.VMEM((width, QUERY_TILE), F32),
            pltpu.VMEM((16, QUERY_TILE), F32),
        ],
        compiler_params=pltpu.CompilerParams(vmem_limit_bytes=VMEM_LIMIT),
        cost_estimate=pl.CostEstimate(
            flops=10 * own * rows * width, bytes_accessed=int(rows * width * 16), transcendentals=own * rows * H // 2
        ),
        name="attend_back",
    )(ids, q, grad_mixed, k_own, k_edge, v_own, v_edge, id_col, id_row, out_t, lse,
      row_col, col_col, row_col, col_col, table)


def ffn_kernel(n2_ref, g_ref, up_ref, b_ref, down_ref, hidden_ref, grad_ref, out_ref, back_ref, sums_ref, out_sc, back_sc):
    step = pl.program_id(0)

    @pl.when(step == 0)
    def _():
        out_sc[...] = jnp.zeros(out_sc.shape, F32)
        back_sc[...] = jnp.zeros(back_sc.shape, F32)

    rows = n2_ref.shape[0]
    block = 256
    sums_ref[...] = jnp.zeros(sums_ref.shape, F32)

    @pl.loop(0, rows // block)
    def _(i):
        here = pl.ds(pl.multiple_of(i * block, block), block)
        pre = dot(n2_ref[here, :], up_ref[...]) + b_ref[...]
        grad_hidden = dot_nt(g_ref[here, :], down_ref[...])
        phi = 0.5 * (1.0 + lax.erf(pre * (0.5 ** 0.5)))
        hidden = (pre * phi).astype(BF)
        slope = phi + pre * (jnp.exp(pre * pre * (-0.5)) * 0.3989422804014327)
        grad_pre = (grad_hidden * slope).astype(BF)
        hidden_ref[here, :] = hidden
        grad_ref[here, :] = grad_pre
        out_sc[here, :] += dot(hidden, down_ref[...])
        back_sc[here, :] += dot_nt(grad_pre, up_ref[...])
        sums_ref[0:1, :] += jnp.sum(grad_pre.astype(F32), axis=0, keepdims=True)

    @pl.when(step == pl.num_programs(0) - 1)
    def _():
        out_ref[...] = out_sc[...].astype(out_ref.dtype)
        back_ref[...] = back_sc[...].astype(back_ref.dtype)


def ffn(n2, g, w_up, b_up, w_down, dtype):
    rows, width = n2.shape
    units = w_up.shape[1]
    block = 256
    whole = pl.BlockSpec((rows, width), lambda j: (0, 0))
    across = pl.BlockSpec((rows, block), lambda j: (0, j))
    return pl.pallas_call(
        ffn_kernel,
        grid=(units // block,),
        in_specs=[
            whole, whole,
            pl.BlockSpec((width, block), lambda j: (0, j)),
            pl.BlockSpec((1, block), lambda j: (0, j)),
            pl.BlockSpec((block, width), lambda j: (j, 0)),
        ],
        out_specs=[across, across, whole, whole, pl.BlockSpec((8, block), lambda j: (0, j))],
        out_shape=[
            jax.ShapeDtypeStruct((rows, units), BF),
            jax.ShapeDtypeStruct((rows, units), BF),
            jax.ShapeDtypeStruct((rows, width), dtype),
            jax.ShapeDtypeStruct((rows, width), dtype),
            jax.ShapeDtypeStruct((8, units), F32),
        ],
        scratch_shapes=[pltpu.VMEM((rows, width), F32), pltpu.VMEM((rows, width), F32)],
        compiler_params=pltpu.CompilerParams(vmem_limit_bytes=VMEM_LIMIT),
        cost_estimate=pl.CostEstimate(
            flops=8 * rows * width * units, bytes_accessed=int(4 * width * units + 4 * rows * units + 8 * rows * width),
            transcendentals=2 * rows * units,
        ),
        name="ffn",
    )(n2, g, w_up, b_up, w_down)


def norm_back(values, gain, grad):
    center = values - jnp.mean(values, axis=-1, keepdims=True)
    inverse = lax.rsqrt(jnp.mean(center * center, axis=-1, keepdims=True) + EPSILON)
    unit = center * inverse
    scaled = grad * gain
    first = jnp.mean(scaled, axis=-1, keepdims=True)
    second = jnp.mean(scaled * unit, axis=-1, keepdims=True)
    back = (scaled - first - unit * second) * inverse
    return back, jnp.sum(grad * unit, axis=0), jnp.sum(grad, axis=0)


def per_device(
    axes, patches, image_of_patch, patch_row, patch_col, ln1_gain, ln1_bias, w_qkv, b_qkv, freqs, w_out, b_out,
    ln2_gain, ln2_bias, w_up, b_up, w_down, b_down, out_cotangent,
):
    own, width = patches.shape
    me = lax.axis_index("mlp")
    other = [(0, 1), (1, 0)]
    swap = lambda a: lax.ppermute(a, "mlp", other)
    edge = min(own, EDGE)
    mine_start = jnp.where(me == 0, own - edge, 0)
    edge_start = jnp.where(me == 0, own, own - edge)
    x_edge = swap(lax.dynamic_slice_in_dim(patches, mine_start, edge))
    g_other = swap(out_cotangent)

    def local(a):
        return jnp.concatenate(
            [lax.dynamic_slice_in_dim(a[0], me * own, own), lax.dynamic_slice_in_dim(a[0], edge_start, edge)]
        )

    ids = local(image_of_patch)
    row_pos = local(patch_row)[:, None]
    col_pos = local(patch_col)[:, None]
    id_row = ids[None, :]
    id_col = ids[:, None]
    id_own = id_row[:, :own]
    table = rope_table(freqs)
    gain1, bias1, bias_qkv = ln1_gain[None], ln1_bias[None], b_qkv[None]
    normed, q, k_own, v_own = input_stage(
        patches, row_pos[:own], col_pos[:own], gain1, bias1, w_qkv, bias_qkv, table, True, 256
    )
    normed_edge, k_edge, v_edge = input_stage(
        x_edge, row_pos[own:], col_pos[own:], gain1, bias1, w_qkv, bias_qkv, table, False, edge // 2
    )
    mixed, out_t, lse = attend(id_row, q, k_own, k_edge, v_own, v_edge, id_col, id_own)
    inputs = patches.astype(F32)
    middle = inputs + dot(mixed, w_out) + b_out
    center = middle - jnp.mean(middle, axis=-1, keepdims=True)
    spread = jnp.mean(center * center, axis=-1, keepdims=True)
    normed2 = (center * lax.rsqrt(spread + EPSILON) * ln2_gain + ln2_bias).astype(BF)
    n2_other = swap(normed2)
    bias_up = b_up[None]
    hid_a, gp_a, out_a, back_a, sum_a = ffn(normed2, out_cotangent, w_up, bias_up, w_down, F32)
    hid_b, gp_b, out_b, back_b, sum_b = ffn(n2_other, g_other, w_up, bias_up, w_down, BF)
    back_in = swap(back_b)
    out_in = swap(out_b)
    grad_b_up = sum_a[0] + sum_b[0]
    grad_w_up = (dot_tn(normed2, gp_a) + dot_tn(n2_other, gp_b)).astype(BF)
    grad_w_down = (dot_tn(hid_a, out_cotangent) + dot_tn(hid_b, g_other)).astype(BF)
    block_out = (middle + out_a + out_in.astype(F32) + b_down).astype(BF)
    grad_out = out_cotangent.astype(F32)
    grad_n2 = back_a + back_in.astype(F32)
    from_norm2, grad_ln2_gain, grad_ln2_bias = norm_back(middle, ln2_gain, grad_n2)
    grad_middle = grad_out + from_norm2
    grad_b_down = jnp.sum(grad_out, axis=0)
    grad_attended = grad_middle.astype(BF)
    grad_b_out = jnp.sum(grad_attended.astype(F32), axis=0)
    grad_w_out = dot_tn(mixed, grad_attended).astype(BF)
    grad_mixed = dot_nt(grad_attended, w_out).astype(BF)
    dq, dk, dv, freq, sums = attend_back(
        id_row, q, grad_mixed, k_own, k_edge, v_own, v_edge, id_col, id_own, out_t, lse, row_pos, col_pos, table
    )
    w_q, w_k, w_v = (w_qkv[:, i * width : (i + 1) * width] for i in range(3))
    gn_edge = (dot_nt(dk[own:], w_k) + dot_nt(dv[own:], w_v)).astype(BF)
    gn_in = swap(gn_edge)
    grad_w_qkv = jnp.concatenate(
        [
            dot_tn(normed, dq).astype(BF),
            (dot_tn(normed, dk[:own]) + dot_tn(normed_edge, dk[own:])).astype(BF),
            (dot_tn(normed, dv[:own]) + dot_tn(normed_edge, dv[own:])).astype(BF),
        ],
        axis=1,
    )
    gn = dot_nt(dq, w_q) + dot_nt(dk[:own], w_k) + dot_nt(dv[:own], w_v)
    spread_in = lax.dynamic_update_slice_in_dim(jnp.zeros((own, width), BF), gn_in, mine_start, 0)
    grad_normed = gn + spread_in.astype(F32)
    from_norm1, grad_ln1_gain, grad_ln1_bias = norm_back(inputs, ln1_gain, grad_normed)
    grad_patches = (grad_middle + from_norm1).astype(BF)
    grad_freqs = jnp.sum(freq[:2].reshape(2, H, 2, HD // 2), axis=2)
    small = jnp.concatenate(
        [
            grad_ln1_gain, grad_ln1_bias, sums[:3].reshape(-1), grad_freqs.reshape(-1),
            grad_b_out, grad_ln2_gain, grad_ln2_bias, grad_b_down,
        ]
    )
    everyone = axes + ("mlp",)
    grad_w_up, grad_w_down = lax.psum((grad_w_up, grad_w_down), axes)
    grad_w_out = lax.psum(grad_w_out, everyone)
    grad_w_qkv = lax.psum(grad_w_qkv, everyone)
    units = b_up.shape[0]
    slots = jnp.zeros((2 * units,), F32)
    slots = lax.dynamic_update_slice_in_dim(slots, grad_b_up, me * units, 0)
    total = lax.psum(jnp.concatenate([small, slots]), everyone)
    grad_b_up = lax.dynamic_slice_in_dim(total, small.shape[0] + me * units, units)
    return (
        block_out, grad_patches, total[0:width], total[width : 2 * width], grad_w_qkv.astype(F32),
        total[2 * width : 5 * width], total[5 * width : 6 * width].reshape(2, width // 2), grad_w_out.astype(F32),
        total[6 * width : 7 * width], total[7 * width : 8 * width], total[8 * width : 9 * width],
        grad_w_up.astype(F32), grad_b_up, grad_w_down.astype(F32), total[9 * width : 10 * width],
    )


def solution(mesh):
    rows = P(("dp", "mlp"), None)
    group = P("dp", None)
    in_specs = (rows, group, group, group) + (P(),) * 9 + (P(None, "mlp"), P("mlp"), P("mlp", None), P(), rows)
    out_specs = (rows, rows) + (P(),) * 9 + (P(None, "mlp"), P("mlp"), P("mlp", None), P())
    return jax.shard_map(
        partial(per_device, ("dp",)), mesh=mesh, in_specs=in_specs, out_specs=out_specs, check_vma=False
    )
```

```python
from functools import partial

import jax
import jax.numpy as jnp
from jax import lax
from jax.experimental import pallas as pl
from jax.experimental.pallas import tpu as pltpu
from jax.sharding import PartitionSpec as P

H = 12
HD = 64
PAIRS = H // 2
LANES = 128
EPSILON = 1e-06
MOST = 576
SLOT = 32
KEY_TILE = 128
QUERY_TILE = 256
AHEAD = 3
EDGE = -(-(MOST - 1) // KEY_TILE) * KEY_TILE
VMEM_LIMIT = 60 * 1024 * 1024
BF = jnp.bfloat16
F32 = jnp.float32


def dot(left, right):
    return jnp.dot(left, right, preferred_element_type=F32)


def dot_nt(left, right):
    return lax.dot_general(left, right, (((1,), (1,)), ((), ())), preferred_element_type=F32)


def dot_tn(left, right):
    return lax.dot_general(left, right, (((0,), (0,)), ((), ())), preferred_element_type=F32)


def fill_table(freq_ref, table_ref):
    full = freq_ref.shape[1]
    steps = lax.broadcasted_iota(jnp.int32, (SLOT, full), 0).astype(F32)
    table_ref[...] = jnp.zeros(table_ref.shape, BF)
    for axis in range(2):
        angle = steps * freq_ref[axis : axis + 1, :]
        for kind, values in enumerate((jnp.cos(angle), jnp.sin(angle))):
            first = (2 * axis + kind) * full
            rest = values
            for part in range(3):
                piece = rest.astype(BF)
                start = (3 * axis + part) * SLOT
                table_ref[start : start + SLOT, first : first + full] = piece
                rest = rest - piece.astype(F32)


def one_hot(row_pos, col_pos):
    rows = row_pos.shape[0]
    lane = lax.broadcasted_iota(jnp.int32, (rows, 256), 1)
    part = jnp.where(lane < 6 * SLOT, lane % SLOT, -1)
    return jnp.where(jnp.where(lane < 3 * SLOT, row_pos, col_pos) == part, 1.0, 0.0).astype(BF)


def cos_sin(hot, table, first, width):
    full = H * HD
    parts = [dot(hot, table[:, k * full + first : k * full + first + width]) for k in range(4)]
    cos_r, sin_r, cos_c, sin_c = parts
    cosine = cos_r * cos_c - sin_r * sin_c
    sine = sin_r * cos_c + cos_r * sin_c
    lane_out = lax.broadcasted_iota(jnp.int32, cosine.shape, 1)
    return cosine, jnp.where(lane_out % HD < HD // 2, -sine, sine)


def swap_halves(values):
    lane = lax.broadcasted_iota(jnp.int32, values.shape, 1)
    return jnp.where(
        lane % HD < HD // 2,
        pltpu.roll(values, LANES - HD // 2, 1),
        pltpu.roll(values, HD // 2, 1),
    )


def input_kernel(own, x_ref, row_ref, col_ref, gain_ref, bias_ref, w_ref, b_ref, t_ref, *outs):
    width = x_ref.shape[1]
    if own:
        normed_ref, k_ref, v_ref, cos_ref, sin_ref, q_ref, table_ref = outs

        @pl.when(pl.program_id(0) == 0)
        def _():
            fill_table(t_ref, table_ref)
    else:
        normed_ref, k_ref, v_ref, cos_ref, sin_ref = outs
        q_ref, table_ref = None, t_ref
    values = x_ref[...].astype(F32)
    center = values - jnp.mean(values, axis=-1, keepdims=True)
    spread = jnp.mean(center * center, axis=-1, keepdims=True)
    normed = (center * lax.rsqrt(spread + EPSILON) * gain_ref[...] + bias_ref[...]).astype(BF)
    normed_ref[...] = normed
    hot = one_hot(row_ref[...], col_ref[...])
    wide = 2 * LANES
    for first in range(0, width, wide):
        cosine, sine = cos_sin(hot, table_ref, first, wide)
        cos_ref[:, first : first + wide] = cosine
        sin_ref[:, first : first + wide] = sine
        for kind, out_ref in ((0, q_ref), (1, k_ref)):
            if out_ref is None:
                continue
            start = kind * width + first
            pre = dot(normed, w_ref[:, start : start + wide]) + b_ref[:, start : start + wide]
            for at in range(0, wide, LANES):
                cut = slice(at, at + LANES)
                turned = pre[:, cut] * cosine[:, cut] + swap_halves(pre[:, cut]) * sine[:, cut]
                out_ref[:, first + at : first + at + LANES] = turned.astype(BF)
    v_ref[...] = (dot(normed, w_ref[:, 2 * width :]) + b_ref[:, 2 * width :]).astype(BF)


def input_stage(x, row_col, col_col, gain, bias, w_qkv, b_qkv, table, own, tile):
    rows, width = x.shape
    tiled = lambda cols: pl.BlockSpec((tile, cols), lambda i: (i, 0))
    whole = lambda a: pl.BlockSpec(a.shape, lambda i: (0, 0))
    shape = lambda dtype: jax.ShapeDtypeStruct((rows, width), dtype)
    outs = [tiled(width)] * 5
    shapes = [shape(BF)] * 3 + [shape(F32)] * 2
    if own:
        full_table = jax.ShapeDtypeStruct((256, 4 * width), BF)
        outs = outs + [tiled(width), whole(full_table)]
        shapes = shapes + [shape(BF), full_table]
    return pl.pallas_call(
        partial(input_kernel, own),
        grid=(rows // tile,),
        in_specs=[tiled(width), tiled(1), tiled(1)] + [whole(a) for a in (gain, bias, w_qkv, b_qkv, table)],
        out_specs=outs,
        out_shape=shapes,
        compiler_params=pltpu.CompilerParams(vmem_limit_bytes=VMEM_LIMIT),
        cost_estimate=pl.CostEstimate(
            flops=2 * rows * width * width * (4 if own else 3),
            bytes_accessed=int(w_qkv.size * 2 + rows * width * 2 * 5),
            transcendentals=0,
        ),
        name="ln_qkv_rope",
    )(x, row_col, col_col, gain, bias, w_qkv, b_qkv, table)


def slab(pair):
    return slice(pair * LANES, (pair + 1) * LANES)


def one_head(values, side):
    lane = lax.broadcasted_iota(jnp.int32, values.shape, 1)
    return jnp.where((lane < HD) if side == 0 else (lane >= HD), values, jnp.zeros_like(values))


def visible(ids_ref, query_tile, key_tile):
    q0 = query_tile * QUERY_TILE
    k0 = key_tile * KEY_TILE
    return (ids_ref[0, k0] <= ids_ref[0, q0 + QUERY_TILE - 1]) & (
        ids_ref[0, k0 + KEY_TILE - 1] >= ids_ref[0, q0]
    )


def attend_kernel(ids_ref, q_ref, k_own_ref, k_edge_ref, v_own_ref, v_edge_ref, idk_ref, idq_ref,
                  mixed_ref, out_t_ref, lse_ref, key_sc, value_t_sc, query_sc, peak_sc, total_sc, acc_sc):
    own = k_own_ref.shape[0]
    rows = key_sc.shape[0]
    step = pl.program_id(0)

    @pl.when(step == 0)
    def _():
        key_sc[0:own, :] = k_own_ref[...]
        key_sc[own:rows, :] = k_edge_ref[...]
        for start in range(0, rows, KEY_TILE):
            for pair in range(PAIRS):
                cut = slab(pair)
                if start < own:
                    block = v_own_ref[start : start + KEY_TILE, cut]
                else:
                    block = v_edge_ref[start - own : start - own + KEY_TILE, cut]
                value_t_sc[start // KEY_TILE, cut, :] = jnp.transpose(block.astype(F32)).astype(BF)

    peak_sc[...] = jnp.full(peak_sc.shape, -1e30, F32)
    total_sc[...] = jnp.zeros(total_sc.shape, F32)
    acc_sc[...] = jnp.zeros(acc_sc.shape, F32)
    for head in range(H):
        query_sc[head] = one_head(q_ref[:, slab(head // 2)], head % 2) * BF(HD ** (-0.5))

    @pl.loop(0, rows // KEY_TILE)
    def _(tile):
        @pl.when(visible(ids_ref, step, tile))
        def _():
            k0 = pl.multiple_of(tile * KEY_TILE, KEY_TILE)
            allowed = idk_ref[pl.ds(k0, KEY_TILE), :] == idq_ref[...]
            score = lambda head: dot_nt(key_sc[pl.ds(k0, KEY_TILE), slab(head // 2)], query_sc[head])
            scores = [score(head) for head in range(AHEAD)]
            waiting = None

            def finish(head, fade, expo):
                part = slice(head * HD, (head + 1) * HD)
                acc_sc[part, :] = fade * acc_sc[part, :] + dot(value_t_sc[tile, part, :], expo)

            for head in range(H):
                if head + AHEAD < H:
                    scores.append(score(head + AHEAD))
                masked = jnp.where(allowed, scores[head], -1e30)
                before = peak_sc[head : head + 1, :]
                peak = jnp.maximum(before, jnp.max(masked, axis=0, keepdims=True))
                expo = jnp.exp(masked - peak)
                fade = jnp.exp(before - peak)
                peak_sc[head : head + 1, :] = peak
                total_sc[head : head + 1, :] = fade * total_sc[head : head + 1, :] + jnp.sum(
                    expo, axis=0, keepdims=True
                )
                if waiting is not None:
                    finish(*waiting)
                waiting = (head, fade, expo.astype(BF))
            finish(*waiting)

    lse_ref[...] = peak_sc[...] + jnp.log(jnp.maximum(total_sc[...], 1e-30))
    for head in range(H):
        part = slice(head * HD, (head + 1) * HD)
        acc_sc[part, :] = acc_sc[part, :] / total_sc[head : head + 1, :]
    out_t_ref[...] = acc_sc[...]
    for pair in range(PAIRS):
        cut = slab(pair)
        mixed_ref[:, cut] = jnp.transpose(acc_sc[cut, :]).astype(BF)


def attend(ids, q, k_own, k_edge, v_own, v_edge, id_col, id_row):
    own, width = q.shape
    rows = own + k_edge.shape[0]
    whole = lambda a: pl.BlockSpec(a.shape, lambda i: (0, 0))
    return pl.pallas_call(
        attend_kernel,
        grid=(own // QUERY_TILE,),
        in_specs=[
            pl.BlockSpec(memory_space=pltpu.SMEM),
            pl.BlockSpec((QUERY_TILE, width), lambda i: (i, 0)),
            whole(k_own), whole(k_edge), whole(v_own), whole(v_edge), whole(id_col),
            pl.BlockSpec((1, QUERY_TILE), lambda i: (0, i)),
        ],
        out_specs=[
            pl.BlockSpec((QUERY_TILE, width), lambda i: (i, 0)),
            pl.BlockSpec((width, QUERY_TILE), lambda i: (0, i)),
            pl.BlockSpec((16, QUERY_TILE), lambda i: (0, i)),
        ],
        out_shape=[
            jax.ShapeDtypeStruct((own, width), BF),
            jax.ShapeDtypeStruct((width, own), F32),
            jax.ShapeDtypeStruct((16, own), F32),
        ],
        scratch_shapes=[
            pltpu.VMEM((rows, width), BF),
            pltpu.VMEM((rows // KEY_TILE, width, KEY_TILE), BF),
            pltpu.VMEM((H, QUERY_TILE, LANES), BF),
            pltpu.VMEM((16, QUERY_TILE), F32),
            pltpu.VMEM((16, QUERY_TILE), F32),
            pltpu.VMEM((width, QUERY_TILE), F32),
        ],
        compiler_params=pltpu.CompilerParams(vmem_limit_bytes=VMEM_LIMIT),
        cost_estimate=pl.CostEstimate(
            flops=4 * own * rows * width, bytes_accessed=int(rows * width * 8), transcendentals=own * rows * H // 2
        ),
        name="attend",
    )(ids, q, k_own, k_edge, v_own, v_edge, id_col, id_row)


def unrotate(grad, rotated, cosine, sine):
    lane = lax.broadcasted_iota(jnp.int32, grad.shape, 1)
    turned = swap_halves(rotated)
    angle = grad * jnp.where(lane % HD < HD // 2, -turned, turned)
    return grad * cosine - swap_halves(grad) * sine, angle


def attend_back_kernel(ids_ref, q_ref, g_ref, k_own_ref, k_edge_ref, v_own_ref, v_edge_ref, idk_ref,
                       idq_ref, out_t_ref, lse_ref, row_ref, col_ref, cos_ref, sin_ref, cos_edge_ref, sin_edge_ref,
                       own_ref, edge_ref, sums_ref,
                       key_sc, value_sc, key_t_sc, query_sc, grad_sc, dk_sc, dv_sc, dq_t_sc, delta_sc):
    own, width = k_own_ref.shape
    rows = key_sc.shape[0]
    step = pl.program_id(0)
    scale = HD ** (-0.5)

    @pl.when(step == 0)
    def _():
        key_sc[0:own, :] = k_own_ref[...]
        key_sc[own:rows, :] = k_edge_ref[...]
        value_sc[0:own, :] = v_own_ref[...]
        value_sc[own:rows, :] = v_edge_ref[...]
        for start in range(0, rows, KEY_TILE):
            for pair in range(PAIRS):
                cut = slab(pair)
                if start < own:
                    block = k_own_ref[start : start + KEY_TILE, cut]
                else:
                    block = k_edge_ref[start - own : start - own + KEY_TILE, cut]
                key_t_sc[start // KEY_TILE, cut, :] = jnp.transpose(block.astype(F32)).astype(BF)
        dk_sc[...] = jnp.zeros(dk_sc.shape, F32)
        dv_sc[...] = jnp.zeros(dv_sc.shape, F32)
        sums_ref[...] = jnp.zeros(sums_ref.shape, F32)

    dq_t_sc[...] = jnp.zeros(dq_t_sc.shape, F32)
    for head in range(H):
        query_sc[head] = one_head(q_ref[:, slab(head // 2)], head % 2) * BF(scale)
        grad_sc[head] = one_head(g_ref[:, slab(head // 2)], head % 2)
    for pair in range(PAIRS):
        cut = slab(pair)
        grad_t = jnp.transpose(g_ref[:, cut].astype(F32)) * out_t_ref[cut, :]
        for side in range(2):
            delta_sc[2 * pair + side : 2 * pair + side + 1, :] = jnp.sum(
                grad_t[side * HD : (side + 1) * HD, :], axis=0, keepdims=True
            )

    @pl.loop(0, rows // KEY_TILE)
    def _(tile):
        @pl.when(visible(ids_ref, step, tile))
        def _():
            k0 = pl.multiple_of(tile * KEY_TILE, KEY_TILE)
            allowed = idk_ref[pl.ds(k0, KEY_TILE), :] == idq_ref[...]
            here = pl.ds(k0, KEY_TILE)

            def first(head):
                cut = slab(head // 2)
                return dot_nt(key_sc[here, cut], query_sc[head]), dot_nt(value_sc[here, cut], grad_sc[head])

            def finish(head, weights, grad_s):
                part = slice(head * HD, (head + 1) * HD)
                dq_t_sc[part, :] += dot(key_t_sc[tile, part, :], grad_s)
                return dot(weights, grad_sc[head]), dot(grad_s, query_sc[head])

            started = [first(head) for head in range(AHEAD)]
            ready = []
            sums = []

            def flush(head):
                sums.append(finish(head, *ready[head]))
                if head % 2 == 1:
                    cut = slab(head // 2)
                    dv_sc[here, cut] += sums[head - 1][0] + sums[head][0]
                    dk_sc[here, cut] += sums[head - 1][1] + sums[head][1]

            for head in range(H):
                if head + AHEAD < H:
                    started.append(first(head + AHEAD))
                scores, grad_w = started[head]
                weights = jnp.where(allowed, jnp.exp(scores - lse_ref[head : head + 1, :]), 0.0)
                grad_s = weights * (grad_w - delta_sc[head : head + 1, :])
                ready.append((weights.astype(BF), grad_s.astype(BF)))
                if head > 0:
                    flush(head - 1)
            flush(H - 1)

    def close(grad, rotated, cosine, sine, row_pos, col_pos, line, cut):
        back, angle = unrotate(grad, rotated.astype(F32), cosine, sine)
        back = back.astype(BF)
        sums_ref[3:4, cut] += jnp.sum(angle * row_pos, axis=0, keepdims=True)
        sums_ref[4:5, cut] += jnp.sum(angle * col_pos, axis=0, keepdims=True)
        sums_ref[line : line + 1, cut] += jnp.sum(back.astype(F32), axis=0, keepdims=True)
        return back

    q_here = pl.ds(pl.multiple_of(step * QUERY_TILE, QUERY_TILE), QUERY_TILE)
    row_q = row_ref[q_here, :].astype(F32)
    col_q = col_ref[q_here, :].astype(F32)
    for pair in range(PAIRS):
        cut = slab(pair)
        grad = jnp.transpose(dq_t_sc[cut, :]) * scale
        own_ref[q_here, cut] = close(
            grad, q_ref[:, cut], cos_ref[q_here, cut], sin_ref[q_here, cut], row_q, col_q, 0, cut
        )

    @pl.when(step == pl.num_programs(0) - 1)
    def _():
        def keys_of(count, first, out_ref, k_at, v_at, c_ref, s_ref):
            @pl.loop(0, count // KEY_TILE)
            def _(tile):
                here = pl.ds(pl.multiple_of(tile * KEY_TILE, KEY_TILE), KEY_TILE)
                there = pl.ds(pl.multiple_of(first + tile * KEY_TILE, KEY_TILE), KEY_TILE)
                row_pos = row_ref[there, :].astype(F32)
                col_pos = col_ref[there, :].astype(F32)
                for pair in range(PAIRS):
                    cut = slab(pair)
                    out_ref[here, k_at + pair * LANES : k_at + (pair + 1) * LANES] = close(
                        dk_sc[there, cut], key_sc[there, cut], c_ref[here, cut], s_ref[here, cut],
                        row_pos, col_pos, 1, cut,
                    )
                    grad_v = dv_sc[there, cut].astype(BF)
                    out_ref[here, v_at + pair * LANES : v_at + (pair + 1) * LANES] = grad_v
                    sums_ref[2:3, cut] += jnp.sum(grad_v.astype(F32), axis=0, keepdims=True)

        keys_of(own, 0, own_ref, width, 2 * width, cos_ref, sin_ref)
        keys_of(rows - own, own, edge_ref, 0, width, cos_edge_ref, sin_edge_ref)


def attend_back(ids, q, grad_mixed, k_own, k_edge, v_own, v_edge, id_col, id_row, out_t, lse, row_col, col_col, turns):
    own, width = q.shape
    edge = k_edge.shape[0]
    rows = own + edge
    whole = lambda a: pl.BlockSpec(a.shape, lambda i: (0, 0))
    once = lambda a: pl.BlockSpec(a.shape, lambda i: (0, 0), pipeline_mode=pl.Buffered(1))
    tiled = pl.BlockSpec((QUERY_TILE, width), lambda i: (i, 0))
    across = lambda n: pl.BlockSpec((n, QUERY_TILE), lambda i: (0, i))
    outs = [
        jax.ShapeDtypeStruct((own, 3 * width), BF),
        jax.ShapeDtypeStruct((edge, 2 * width), BF),
        jax.ShapeDtypeStruct((8, width), F32),
    ]
    return pl.pallas_call(
        attend_back_kernel,
        grid=(own // QUERY_TILE,),
        in_specs=[
            pl.BlockSpec(memory_space=pltpu.SMEM), tiled, tiled,
            once(k_own), once(k_edge), once(v_own), once(v_edge), once(id_col),
            across(1), across(width), across(16), once(row_col), once(col_col),
        ] + [once(a) for a in turns],
        out_specs=[whole(a) for a in outs],
        out_shape=outs,
        scratch_shapes=[
            pltpu.VMEM((rows, width), BF),
            pltpu.VMEM((rows, width), BF),
            pltpu.VMEM((rows // KEY_TILE, width, KEY_TILE), BF),
            pltpu.VMEM((H, QUERY_TILE, LANES), BF),
            pltpu.VMEM((H, QUERY_TILE, LANES), BF),
            pltpu.VMEM((rows, width), F32),
            pltpu.VMEM((rows, width), F32),
            pltpu.VMEM((width, QUERY_TILE), F32),
            pltpu.VMEM((16, QUERY_TILE), F32),
        ],
        compiler_params=pltpu.CompilerParams(vmem_limit_bytes=VMEM_LIMIT),
        cost_estimate=pl.CostEstimate(
            flops=10 * own * rows * width, bytes_accessed=int(rows * width * 16), transcendentals=own * rows * H // 2
        ),
        name="attend_back",
    )(ids, q, grad_mixed, k_own, k_edge, v_own, v_edge, id_col, id_row, out_t, lse, row_col, col_col, *turns)


def ffn_kernel(n2_ref, g_ref, up_ref, b_ref, down_ref, hidden_ref, grad_ref, out_ref, back_ref, sums_ref, out_sc, back_sc):
    step = pl.program_id(0)

    @pl.when(step == 0)
    def _():
        out_sc[...] = jnp.zeros(out_sc.shape, F32)
        back_sc[...] = jnp.zeros(back_sc.shape, F32)

    rows = n2_ref.shape[0]
    block = 128
    sums_ref[...] = jnp.zeros(sums_ref.shape, F32)

    cuts = [slice(i, i + block) for i in range(0, rows, block)]

    def first(here):
        return dot(n2_ref[here, :], up_ref[...]) + b_ref[...], dot_nt(g_ref[here, :], down_ref[...])

    def finish(here, hidden, grad_pre):
        out_sc[here, :] += dot(hidden, down_ref[...])
        back_sc[here, :] += dot_nt(grad_pre, up_ref[...])

    started = [first(cuts[0])]
    ready = []
    total = jnp.zeros((1, up_ref.shape[1]), F32)
    for i, here in enumerate(cuts):
        if i + 1 < len(cuts):
            started.append(first(cuts[i + 1]))
        pre, grad_hidden = started[i]
        phi = 0.5 * (1.0 + lax.erf(pre * (0.5 ** 0.5)))
        hidden = (pre * phi).astype(BF)
        slope = phi + pre * (jnp.exp(pre * pre * (-0.5)) * 0.3989422804014327)
        grad_pre = (grad_hidden * slope).astype(BF)
        hidden_ref[here, :] = hidden
        grad_ref[here, :] = grad_pre
        total += jnp.sum(grad_pre.astype(F32), axis=0, keepdims=True)
        ready.append((hidden, grad_pre))
        if i > 0:
            finish(cuts[i - 1], *ready[i - 1])
    finish(cuts[-1], *ready[-1])
    sums_ref[0:1, :] = total

    @pl.when(step == pl.num_programs(0) - 1)
    def _():
        out_ref[...] = out_sc[...].astype(out_ref.dtype)
        back_ref[...] = back_sc[...].astype(back_ref.dtype)


def ffn(n2, g, w_up, b_up, w_down, dtype):
    rows, width = n2.shape
    units = w_up.shape[1]
    block = 256
    whole = pl.BlockSpec((rows, width), lambda j: (0, 0))
    across = pl.BlockSpec((rows, block), lambda j: (0, j))
    return pl.pallas_call(
        ffn_kernel,
        grid=(units // block,),
        in_specs=[
            whole, whole,
            pl.BlockSpec((width, block), lambda j: (0, j)),
            pl.BlockSpec((1, block), lambda j: (0, j)),
            pl.BlockSpec((block, width), lambda j: (j, 0)),
        ],
        out_specs=[across, across, whole, whole, pl.BlockSpec((8, block), lambda j: (0, j))],
        out_shape=[
            jax.ShapeDtypeStruct((rows, units), BF),
            jax.ShapeDtypeStruct((rows, units), BF),
            jax.ShapeDtypeStruct((rows, width), dtype),
            jax.ShapeDtypeStruct((rows, width), dtype),
            jax.ShapeDtypeStruct((8, units), F32),
        ],
        scratch_shapes=[pltpu.VMEM((rows, width), F32), pltpu.VMEM((rows, width), F32)],
        compiler_params=pltpu.CompilerParams(vmem_limit_bytes=VMEM_LIMIT),
        cost_estimate=pl.CostEstimate(
            flops=8 * rows * width * units, bytes_accessed=int(4 * width * units + 4 * rows * units + 8 * rows * width),
            transcendentals=2 * rows * units,
        ),
        name="ffn",
    )(n2, g, w_up, b_up, w_down)


def norm_back(values, gain, grad):
    center = values - jnp.mean(values, axis=-1, keepdims=True)
    inverse = lax.rsqrt(jnp.mean(center * center, axis=-1, keepdims=True) + EPSILON)
    unit = center * inverse
    scaled = grad * gain
    first = jnp.mean(scaled, axis=-1, keepdims=True)
    second = jnp.mean(scaled * unit, axis=-1, keepdims=True)
    back = (scaled - first - unit * second) * inverse
    return back, jnp.sum(grad * unit, axis=0), jnp.sum(grad, axis=0)


def per_device(
    axes, patches, image_of_patch, patch_row, patch_col, ln1_gain, ln1_bias, w_qkv, b_qkv, freqs, w_out, b_out,
    ln2_gain, ln2_bias, w_up, b_up, w_down, b_down, out_cotangent,
):
    own, width = patches.shape
    me = lax.axis_index("mlp")
    other = [(0, 1), (1, 0)]
    swap = lambda a: lax.ppermute(a, "mlp", other)
    edge = min(own, EDGE)
    mine_start = jnp.where(me == 0, own - edge, 0)
    edge_start = jnp.where(me == 0, own, own - edge)
    x_edge = swap(lax.dynamic_slice_in_dim(patches, mine_start, edge))
    g_other = swap(out_cotangent)

    def local(a):
        return jnp.concatenate(
            [lax.dynamic_slice_in_dim(a[0], me * own, own), lax.dynamic_slice_in_dim(a[0], edge_start, edge)]
        )

    ids = local(image_of_patch)
    row_pos = local(patch_row)[:, None]
    col_pos = local(patch_col)[:, None]
    id_row = ids[None, :]
    id_col = ids[:, None]
    id_own = id_row[:, :own]
    wide_freqs = jnp.concatenate([freqs.reshape(2, H, 1, HD // 2)] * 2, axis=2).reshape(2, width)
    gain1, bias1, bias_qkv = ln1_gain[None], ln1_bias[None], b_qkv[None]
    normed, k_own, v_own, cos_own, sin_own, q, table = input_stage(
        patches, row_pos[:own], col_pos[:own], gain1, bias1, w_qkv, bias_qkv, wide_freqs, True, 256
    )
    normed_edge, k_edge, v_edge, cos_edge, sin_edge = input_stage(
        x_edge, row_pos[own:], col_pos[own:], gain1, bias1, w_qkv, bias_qkv, table, False, edge // 2
    )
    mixed, out_t, lse = attend(id_row, q, k_own, k_edge, v_own, v_edge, id_col, id_own)
    inputs = patches.astype(F32)
    middle = inputs + dot(mixed, w_out) + b_out
    center = middle - jnp.mean(middle, axis=-1, keepdims=True)
    spread = jnp.mean(center * center, axis=-1, keepdims=True)
    normed2 = (center * lax.rsqrt(spread + EPSILON) * ln2_gain + ln2_bias).astype(BF)
    n2_other = swap(normed2)
    bias_up = b_up[None]
    hid_a, gp_a, out_a, back_a, sum_a = ffn(normed2, out_cotangent, w_up, bias_up, w_down, F32)
    hid_b, gp_b, out_b, back_b, sum_b = ffn(n2_other, g_other, w_up, bias_up, w_down, BF)
    back_in = swap(back_b)
    out_in = swap(out_b)
    grad_b_up = sum_a[0] + sum_b[0]
    grad_w_up = (dot_tn(normed2, gp_a) + dot_tn(n2_other, gp_b)).astype(BF)
    grad_w_down = (dot_tn(hid_a, out_cotangent) + dot_tn(hid_b, g_other)).astype(BF)
    block_out = (middle + out_a + out_in.astype(F32) + b_down).astype(BF)
    grad_out = out_cotangent.astype(F32)
    grad_n2 = back_a + back_in.astype(F32)
    from_norm2, grad_ln2_gain, grad_ln2_bias = norm_back(middle, ln2_gain, grad_n2)
    grad_middle = grad_out + from_norm2
    grad_b_down = jnp.sum(grad_out, axis=0)
    grad_attended = grad_middle.astype(BF)
    grad_b_out = jnp.sum(grad_attended.astype(F32), axis=0)
    grad_w_out = dot_tn(mixed, grad_attended).astype(BF)
    grad_mixed = dot_nt(grad_attended, w_out).astype(BF)
    d_own, d_edge, sums = attend_back(
        id_row, q, grad_mixed, k_own, k_edge, v_own, v_edge, id_col, id_own, out_t, lse, row_pos, col_pos,
        (cos_own, sin_own, cos_edge, sin_edge),
    )
    gn_in = swap(dot_nt(d_edge, w_qkv[:, width:]).astype(BF))
    grad_w_q = dot_tn(normed, d_own[:, :width]).astype(BF)
    grad_w_kv = (dot_tn(normed, d_own[:, width:]) + dot_tn(normed_edge, d_edge)).astype(BF)
    gn = dot_nt(d_own, w_qkv)
    spread_in = lax.dynamic_update_slice_in_dim(jnp.zeros((own, width), BF), gn_in, mine_start, 0)
    grad_normed = gn + spread_in.astype(F32)
    from_norm1, grad_ln1_gain, grad_ln1_bias = norm_back(inputs, ln1_gain, grad_normed)
    grad_patches = (grad_middle + from_norm1).astype(BF)
    everyone = axes + ("mlp",)
    units = b_up.shape[0] // width
    lines = [grad_ln1_gain, grad_ln1_bias] + [sums[i] for i in range(5)]
    lines += [grad_b_out, grad_ln2_gain, grad_ln2_bias, grad_b_down]
    count = len(lines)
    line = lax.broadcasted_iota(jnp.int32, (16, width), 0)
    small = jnp.zeros((16, width), F32)
    for i, values in enumerate(lines):
        small = jnp.where(line == i, values[None], small)
    for i in range(units):
        small = jnp.where(line == count + me * units + i, grad_b_up[None, i * width : (i + 1) * width], small)
    grad_w_up, grad_w_down = lax.psum((grad_w_up, grad_w_down), axes)
    grad_w_q, grad_w_kv, grad_w_out = lax.psum((grad_w_q, grad_w_kv, grad_w_out), everyone)
    total = lax.psum(small, everyone)
    grad_b_up = lax.dynamic_slice_in_dim(total, count + me * units, units).reshape(units * width)
    grad_w_qkv = jnp.concatenate([grad_w_q, grad_w_kv], axis=1).astype(F32)
    grad_freqs = jnp.sum(total[5:7].reshape(2, H, 2, HD // 2), axis=2).reshape(2, width // 2)
    total = [total[i] for i in range(count)]
    return (
        block_out, grad_patches, total[0], total[1], grad_w_qkv, jnp.concatenate(total[2:5]), grad_freqs,
        grad_w_out.astype(F32), total[7], total[8], total[9], grad_w_up.astype(F32), grad_b_up,
        grad_w_down.astype(F32), total[10],
    )


def solution(mesh):
    rows = P(("dp", "mlp"), None)
    group = P("dp", None)
    in_specs = (rows, group, group, group) + (P(),) * 9 + (P(None, "mlp"), P("mlp"), P("mlp", None), P(), rows)
    out_specs = (rows, rows) + (P(),) * 9 + (P(None, "mlp"), P("mlp"), P("mlp", None), P())
    return jax.shard_map(
        partial(per_device, ("dp",)), mesh=mesh, in_specs=in_specs, out_specs=out_specs, check_vma=False
    )
```

```python
from functools import partial

import jax
import jax.numpy as jnp
from jax import lax
from jax.experimental import pallas as pl
from jax.experimental.pallas import tpu as pltpu
from jax.sharding import PartitionSpec as P

H = 12
HD = 64
PAIRS = H // 2
LANES = 128
EPSILON = 1e-06
MOST = 576
SLOT = 32
KEY_TILE = 128
QUERY_TILE = 256
AHEAD = 3
EDGE = -(-(MOST - 1) // KEY_TILE) * KEY_TILE
VMEM_LIMIT = 60 * 1024 * 1024
BF = jnp.bfloat16
F32 = jnp.float32


def dot(left, right):
    return jnp.dot(left, right, preferred_element_type=F32)


def dot_nt(left, right):
    return lax.dot_general(left, right, (((1,), (1,)), ((), ())), preferred_element_type=F32)


def dot_tn(left, right):
    return lax.dot_general(left, right, (((0,), (0,)), ((), ())), preferred_element_type=F32)


def fill_table(freq_ref, table_ref):
    full = freq_ref.shape[1]
    steps = lax.broadcasted_iota(jnp.int32, (SLOT, full), 0).astype(F32)
    table_ref[...] = jnp.zeros(table_ref.shape, BF)
    for axis in range(2):
        angle = steps * freq_ref[axis : axis + 1, :]
        for kind, values in enumerate((jnp.cos(angle), jnp.sin(angle))):
            first = (2 * axis + kind) * full
            rest = values
            for part in range(3):
                piece = rest.astype(BF)
                start = (3 * axis + part) * SLOT
                table_ref[start : start + SLOT, first : first + full] = piece
                rest = rest - piece.astype(F32)


def one_hot(row_pos, col_pos):
    rows = row_pos.shape[0]
    lane = lax.broadcasted_iota(jnp.int32, (rows, 256), 1)
    part = jnp.where(lane < 6 * SLOT, lane % SLOT, -1)
    return jnp.where(jnp.where(lane < 3 * SLOT, row_pos, col_pos) == part, 1.0, 0.0).astype(BF)


def cos_sin(hot, table, first, width):
    full = H * HD
    parts = [dot(hot, table[:, k * full + first : k * full + first + width]) for k in range(4)]
    cos_r, sin_r, cos_c, sin_c = parts
    cosine = cos_r * cos_c - sin_r * sin_c
    sine = sin_r * cos_c + cos_r * sin_c
    lane_out = lax.broadcasted_iota(jnp.int32, cosine.shape, 1)
    return cosine, jnp.where(lane_out % HD < HD // 2, -sine, sine)


def swap_halves(values):
    lane = lax.broadcasted_iota(jnp.int32, values.shape, 1)
    return jnp.where(
        lane % HD < HD // 2,
        pltpu.roll(values, LANES - HD // 2, 1),
        pltpu.roll(values, HD // 2, 1),
    )


def input_kernel(own, x_ref, row_ref, col_ref, gain_ref, bias_ref, w_ref, b_ref, t_ref, *outs):
    width = x_ref.shape[1]
    if own:
        normed_ref, k_ref, v_ref, cos_ref, sin_ref, q_ref, table_ref = outs

        @pl.when(pl.program_id(0) == 0)
        def _():
            fill_table(t_ref, table_ref)
    else:
        normed_ref, k_ref, v_ref, cos_ref, sin_ref = outs
        q_ref, table_ref = None, t_ref
    values = x_ref[...].astype(F32)
    center = values - jnp.mean(values, axis=-1, keepdims=True)
    spread = jnp.mean(center * center, axis=-1, keepdims=True)
    normed = (center * lax.rsqrt(spread + EPSILON) * gain_ref[...] + bias_ref[...]).astype(BF)
    normed_ref[...] = normed
    hot = one_hot(row_ref[...], col_ref[...])
    wide = 2 * LANES
    for first in range(0, width, wide):
        cosine, sine = cos_sin(hot, table_ref, first, wide)
        cos_ref[:, first : first + wide] = cosine
        sin_ref[:, first : first + wide] = sine
        for kind, out_ref in ((0, q_ref), (1, k_ref)):
            if out_ref is None:
                continue
            start = kind * width + first
            pre = dot(normed, w_ref[:, start : start + wide]) + b_ref[:, start : start + wide]
            for at in range(0, wide, LANES):
                cut = slice(at, at + LANES)
                turned = pre[:, cut] * cosine[:, cut] + swap_halves(pre[:, cut]) * sine[:, cut]
                out_ref[:, first + at : first + at + LANES] = turned.astype(BF)
    v_ref[...] = (dot(normed, w_ref[:, 2 * width :]) + b_ref[:, 2 * width :]).astype(BF)


def input_stage(x, row_col, col_col, gain, bias, w_qkv, b_qkv, table, own, tile):
    rows, width = x.shape
    tiled = lambda cols: pl.BlockSpec((tile, cols), lambda i: (i, 0))
    whole = lambda a: pl.BlockSpec(a.shape, lambda i: (0, 0))
    shape = lambda dtype: jax.ShapeDtypeStruct((rows, width), dtype)
    outs = [tiled(width)] * 5
    shapes = [shape(BF)] * 3 + [shape(F32)] * 2
    if own:
        full_table = jax.ShapeDtypeStruct((256, 4 * width), BF)
        outs = outs + [tiled(width), whole(full_table)]
        shapes = shapes + [shape(BF), full_table]
    return pl.pallas_call(
        partial(input_kernel, own),
        grid=(rows // tile,),
        in_specs=[tiled(width), tiled(1), tiled(1)] + [whole(a) for a in (gain, bias, w_qkv, b_qkv, table)],
        out_specs=outs,
        out_shape=shapes,
        compiler_params=pltpu.CompilerParams(vmem_limit_bytes=VMEM_LIMIT),
        cost_estimate=pl.CostEstimate(
            flops=2 * rows * width * width * (4 if own else 3),
            bytes_accessed=int(w_qkv.size * 2 + rows * width * 2 * 5),
            transcendentals=0,
        ),
        name="ln_qkv_rope",
    )(x, row_col, col_col, gain, bias, w_qkv, b_qkv, table)


def slab(pair):
    return slice(pair * LANES, (pair + 1) * LANES)


def one_head(values, side):
    lane = lax.broadcasted_iota(jnp.int32, values.shape, 1)
    return jnp.where((lane < HD) if side == 0 else (lane >= HD), values, jnp.zeros_like(values))


def visible(ids_ref, query_tile, key_tile):
    q0 = query_tile * QUERY_TILE
    k0 = key_tile * KEY_TILE
    return (ids_ref[0, k0] <= ids_ref[0, q0 + QUERY_TILE - 1]) & (
        ids_ref[0, k0 + KEY_TILE - 1] >= ids_ref[0, q0]
    )


def attend_kernel(ids_ref, q_ref, k_own_ref, k_edge_ref, v_own_ref, v_edge_ref, idk_ref, idq_ref,
                  mixed_ref, out_t_ref, lse_ref, key_sc, value_t_sc, query_sc, peak_sc, total_sc, acc_sc):
    own = k_own_ref.shape[0]
    rows = key_sc.shape[0]
    step = pl.program_id(0)

    @pl.when(step == 0)
    def _():
        key_sc[0:own, :] = k_own_ref[...]
        key_sc[own:rows, :] = k_edge_ref[...]
        for start in range(0, rows, KEY_TILE):
            for pair in range(PAIRS):
                cut = slab(pair)
                if start < own:
                    block = v_own_ref[start : start + KEY_TILE, cut]
                else:
                    block = v_edge_ref[start - own : start - own + KEY_TILE, cut]
                value_t_sc[start // KEY_TILE, cut, :] = jnp.transpose(block.astype(F32)).astype(BF)

    peak_sc[...] = jnp.full(peak_sc.shape, -1e30, F32)
    total_sc[...] = jnp.zeros(total_sc.shape, F32)
    acc_sc[...] = jnp.zeros(acc_sc.shape, F32)
    for head in range(H):
        query_sc[head] = one_head(q_ref[:, slab(head // 2)], head % 2) * BF(HD ** (-0.5))

    @pl.loop(0, rows // KEY_TILE)
    def _(tile):
        @pl.when(visible(ids_ref, step, tile))
        def _():
            k0 = pl.multiple_of(tile * KEY_TILE, KEY_TILE)
            allowed = idk_ref[pl.ds(k0, KEY_TILE), :] == idq_ref[...]
            score = lambda head: dot_nt(key_sc[pl.ds(k0, KEY_TILE), slab(head // 2)], query_sc[head])
            scores = [score(head) for head in range(AHEAD)]
            waiting = None

            def finish(head, fade, expo):
                part = slice(head * HD, (head + 1) * HD)
                acc_sc[part, :] = fade * acc_sc[part, :] + dot(value_t_sc[tile, part, :], expo)

            for head in range(H):
                if head + AHEAD < H:
                    scores.append(score(head + AHEAD))
                masked = jnp.where(allowed, scores[head], -1e30)
                before = peak_sc[head : head + 1, :]
                peak = jnp.maximum(before, jnp.max(masked, axis=0, keepdims=True))
                expo = jnp.exp(masked - peak)
                fade = jnp.exp(before - peak)
                peak_sc[head : head + 1, :] = peak
                total_sc[head : head + 1, :] = fade * total_sc[head : head + 1, :] + jnp.sum(
                    expo, axis=0, keepdims=True
                )
                if waiting is not None:
                    finish(*waiting)
                waiting = (head, fade, expo.astype(BF))
            finish(*waiting)

    lse_ref[...] = peak_sc[...] + jnp.log(jnp.maximum(total_sc[...], 1e-30))
    for head in range(H):
        part = slice(head * HD, (head + 1) * HD)
        acc_sc[part, :] = acc_sc[part, :] / total_sc[head : head + 1, :]
    out_t_ref[...] = acc_sc[...]
    for pair in range(PAIRS):
        cut = slab(pair)
        mixed_ref[:, cut] = jnp.transpose(acc_sc[cut, :]).astype(BF)


def attend(ids, q, k_own, k_edge, v_own, v_edge, id_col, id_row):
    own, width = q.shape
    rows = own + k_edge.shape[0]
    whole = lambda a: pl.BlockSpec(a.shape, lambda i: (0, 0))
    return pl.pallas_call(
        attend_kernel,
        grid=(own // QUERY_TILE,),
        in_specs=[
            pl.BlockSpec(memory_space=pltpu.SMEM),
            pl.BlockSpec((QUERY_TILE, width), lambda i: (i, 0)),
            whole(k_own), whole(k_edge), whole(v_own), whole(v_edge), whole(id_col),
            pl.BlockSpec((1, QUERY_TILE), lambda i: (0, i)),
        ],
        out_specs=[
            pl.BlockSpec((QUERY_TILE, width), lambda i: (i, 0)),
            pl.BlockSpec((width, QUERY_TILE), lambda i: (0, i)),
            pl.BlockSpec((16, QUERY_TILE), lambda i: (0, i)),
        ],
        out_shape=[
            jax.ShapeDtypeStruct((own, width), BF),
            jax.ShapeDtypeStruct((width, own), F32),
            jax.ShapeDtypeStruct((16, own), F32),
        ],
        scratch_shapes=[
            pltpu.VMEM((rows, width), BF),
            pltpu.VMEM((rows // KEY_TILE, width, KEY_TILE), BF),
            pltpu.VMEM((H, QUERY_TILE, LANES), BF),
            pltpu.VMEM((16, QUERY_TILE), F32),
            pltpu.VMEM((16, QUERY_TILE), F32),
            pltpu.VMEM((width, QUERY_TILE), F32),
        ],
        compiler_params=pltpu.CompilerParams(vmem_limit_bytes=VMEM_LIMIT),
        cost_estimate=pl.CostEstimate(
            flops=4 * own * rows * width, bytes_accessed=int(rows * width * 8), transcendentals=own * rows * H // 2
        ),
        name="attend",
    )(ids, q, k_own, k_edge, v_own, v_edge, id_col, id_row)


def unrotate(grad, rotated, cosine, sine):
    lane = lax.broadcasted_iota(jnp.int32, grad.shape, 1)
    turned = swap_halves(rotated)
    angle = grad * jnp.where(lane % HD < HD // 2, -turned, turned)
    return grad * cosine - swap_halves(grad) * sine, angle


def attend_back_kernel(ids_ref, q_ref, g_ref, k_own_ref, k_edge_ref, v_own_ref, v_edge_ref, idk_ref,
                       idq_ref, out_t_ref, lse_ref, row_ref, col_ref, cos_ref, sin_ref, cos_edge_ref, sin_edge_ref,
                       own_ref, edge_ref, sums_ref,
                       key_sc, value_sc, key_t_sc, query_sc, grad_sc, dk_sc, dv_sc, dq_t_sc, delta_sc):
    own, width = k_own_ref.shape
    rows = key_sc.shape[0]
    step = pl.program_id(0)
    scale = HD ** (-0.5)

    @pl.when(step == 0)
    def _():
        key_sc[0:own, :] = k_own_ref[...]
        key_sc[own:rows, :] = k_edge_ref[...]
        value_sc[0:own, :] = v_own_ref[...]
        value_sc[own:rows, :] = v_edge_ref[...]
        for start in range(0, rows, KEY_TILE):
            for pair in range(PAIRS):
                cut = slab(pair)
                if start < own:
                    block = k_own_ref[start : start + KEY_TILE, cut]
                else:
                    block = k_edge_ref[start - own : start - own + KEY_TILE, cut]
                key_t_sc[start // KEY_TILE, cut, :] = jnp.transpose(block.astype(F32)).astype(BF)
        dk_sc[...] = jnp.zeros(dk_sc.shape, F32)
        dv_sc[...] = jnp.zeros(dv_sc.shape, F32)
        sums_ref[...] = jnp.zeros(sums_ref.shape, F32)

    dq_t_sc[...] = jnp.zeros(dq_t_sc.shape, F32)
    for head in range(H):
        query_sc[head] = one_head(q_ref[:, slab(head // 2)], head % 2) * BF(scale)
        grad_sc[head] = one_head(g_ref[:, slab(head // 2)], head % 2)
    for pair in range(PAIRS):
        cut = slab(pair)
        grad_t = jnp.transpose(g_ref[:, cut].astype(F32)) * out_t_ref[cut, :]
        for side in range(2):
            delta_sc[2 * pair + side : 2 * pair + side + 1, :] = jnp.sum(
                grad_t[side * HD : (side + 1) * HD, :], axis=0, keepdims=True
            )

    @pl.loop(0, rows // KEY_TILE)
    def _(tile):
        @pl.when(visible(ids_ref, step, tile))
        def _():
            k0 = pl.multiple_of(tile * KEY_TILE, KEY_TILE)
            allowed = idk_ref[pl.ds(k0, KEY_TILE), :] == idq_ref[...]
            here = pl.ds(k0, KEY_TILE)

            def first(head):
                cut = slab(head // 2)
                return dot_nt(key_sc[here, cut], query_sc[head]), dot_nt(value_sc[here, cut], grad_sc[head])

            def finish(head, weights, grad_s):
                part = slice(head * HD, (head + 1) * HD)
                dq_t_sc[part, :] += dot(key_t_sc[tile, part, :], grad_s)
                return dot(weights, grad_sc[head]), dot(grad_s, query_sc[head])

            started = [first(head) for head in range(AHEAD)]
            ready = []
            sums = []

            def flush(head):
                sums.append(finish(head, *ready[head]))
                if head % 2 == 1:
                    cut = slab(head // 2)
                    dv_sc[here, cut] += sums[head - 1][0] + sums[head][0]
                    dk_sc[here, cut] += sums[head - 1][1] + sums[head][1]

            for head in range(H):
                if head + AHEAD < H:
                    started.append(first(head + AHEAD))
                scores, grad_w = started[head]
                weights = jnp.where(allowed, jnp.exp(scores - lse_ref[head : head + 1, :]), 0.0)
                grad_s = weights * (grad_w - delta_sc[head : head + 1, :])
                ready.append((weights.astype(BF), grad_s.astype(BF)))
                if head > 0:
                    flush(head - 1)
            flush(H - 1)

    def close(grad, rotated, cosine, sine, row_pos, col_pos, line, cut):
        back, angle = unrotate(grad, rotated.astype(F32), cosine, sine)
        back = back.astype(BF)
        sums_ref[3:4, cut] += jnp.sum(angle * row_pos, axis=0, keepdims=True)
        sums_ref[4:5, cut] += jnp.sum(angle * col_pos, axis=0, keepdims=True)
        sums_ref[line : line + 1, cut] += jnp.sum(back.astype(F32), axis=0, keepdims=True)
        return back

    q_here = pl.ds(pl.multiple_of(step * QUERY_TILE, QUERY_TILE), QUERY_TILE)
    row_q = row_ref[q_here, :].astype(F32)
    col_q = col_ref[q_here, :].astype(F32)
    for pair in range(PAIRS):
        cut = slab(pair)
        grad = jnp.transpose(dq_t_sc[cut, :]) * scale
        own_ref[q_here, cut] = close(
            grad, q_ref[:, cut], cos_ref[q_here, cut], sin_ref[q_here, cut], row_q, col_q, 0, cut
        )

    @pl.when(step == pl.num_programs(0) - 1)
    def _():
        def keys_of(count, first, out_ref, k_at, v_at, c_ref, s_ref):
            @pl.loop(0, count // KEY_TILE)
            def _(tile):
                here = pl.ds(pl.multiple_of(tile * KEY_TILE, KEY_TILE), KEY_TILE)
                there = pl.ds(pl.multiple_of(first + tile * KEY_TILE, KEY_TILE), KEY_TILE)
                row_pos = row_ref[there, :].astype(F32)
                col_pos = col_ref[there, :].astype(F32)
                for pair in range(PAIRS):
                    cut = slab(pair)
                    out_ref[here, k_at + pair * LANES : k_at + (pair + 1) * LANES] = close(
                        dk_sc[there, cut], key_sc[there, cut], c_ref[here, cut], s_ref[here, cut],
                        row_pos, col_pos, 1, cut,
                    )
                    grad_v = dv_sc[there, cut].astype(BF)
                    out_ref[here, v_at + pair * LANES : v_at + (pair + 1) * LANES] = grad_v
                    sums_ref[2:3, cut] += jnp.sum(grad_v.astype(F32), axis=0, keepdims=True)

        keys_of(own, 0, own_ref, width, 2 * width, cos_ref, sin_ref)
        keys_of(rows - own, own, edge_ref, 0, width, cos_edge_ref, sin_edge_ref)


def attend_back(ids, q, grad_mixed, k_own, k_edge, v_own, v_edge, id_col, id_row, out_t, lse, row_col, col_col, turns):
    own, width = q.shape
    edge = k_edge.shape[0]
    rows = own + edge
    whole = lambda a: pl.BlockSpec(a.shape, lambda i: (0, 0))
    once = lambda a: pl.BlockSpec(a.shape, lambda i: (0, 0), pipeline_mode=pl.Buffered(1))
    tiled = pl.BlockSpec((QUERY_TILE, width), lambda i: (i, 0))
    across = lambda n: pl.BlockSpec((n, QUERY_TILE), lambda i: (0, i))
    outs = [
        jax.ShapeDtypeStruct((own, 3 * width), BF),
        jax.ShapeDtypeStruct((edge, 2 * width), BF),
        jax.ShapeDtypeStruct((8, width), F32),
    ]
    return pl.pallas_call(
        attend_back_kernel,
        grid=(own // QUERY_TILE,),
        in_specs=[
            pl.BlockSpec(memory_space=pltpu.SMEM), tiled, tiled,
            once(k_own), once(k_edge), once(v_own), once(v_edge), once(id_col),
            across(1), across(width), across(16), once(row_col), once(col_col),
        ] + [once(a) for a in turns],
        out_specs=[whole(a) for a in outs],
        out_shape=outs,
        scratch_shapes=[
            pltpu.VMEM((rows, width), BF),
            pltpu.VMEM((rows, width), BF),
            pltpu.VMEM((rows // KEY_TILE, width, KEY_TILE), BF),
            pltpu.VMEM((H, QUERY_TILE, LANES), BF),
            pltpu.VMEM((H, QUERY_TILE, LANES), BF),
            pltpu.VMEM((rows, width), F32),
            pltpu.VMEM((rows, width), F32),
            pltpu.VMEM((width, QUERY_TILE), F32),
            pltpu.VMEM((16, QUERY_TILE), F32),
        ],
        compiler_params=pltpu.CompilerParams(vmem_limit_bytes=VMEM_LIMIT),
        cost_estimate=pl.CostEstimate(
            flops=10 * own * rows * width, bytes_accessed=int(rows * width * 16), transcendentals=own * rows * H // 2
        ),
        name="attend_back",
    )(ids, q, grad_mixed, k_own, k_edge, v_own, v_edge, id_col, id_row, out_t, lse, row_col, col_col, *turns)


def ffn_kernel(n2_ref, g_ref, up_ref, b_ref, down_ref, hidden_ref, grad_ref, out_ref, back_ref, sums_ref, out_sc, back_sc):
    step = pl.program_id(0)

    @pl.when(step == 0)
    def _():
        out_sc[...] = jnp.zeros(out_sc.shape, F32)
        back_sc[...] = jnp.zeros(back_sc.shape, F32)

    rows = n2_ref.shape[0]
    block = 128
    sums_ref[...] = jnp.zeros(sums_ref.shape, F32)

    cuts = [slice(i, i + block) for i in range(0, rows, block)]

    def first(here):
        return dot(n2_ref[here, :], up_ref[...]) + b_ref[...], dot_nt(g_ref[here, :], down_ref[...])

    def finish(here, hidden, grad_pre):
        out_sc[here, :] += dot(hidden, down_ref[...])
        back_sc[here, :] += dot_nt(grad_pre, up_ref[...])

    started = [first(cuts[0])]
    ready = []
    total = jnp.zeros((1, up_ref.shape[1]), F32)
    for i, here in enumerate(cuts):
        if i + 1 < len(cuts):
            started.append(first(cuts[i + 1]))
        pre, grad_hidden = started[i]
        phi = 0.5 * (1.0 + lax.erf(pre * (0.5 ** 0.5)))
        hidden = (pre * phi).astype(BF)
        slope = phi + pre * (jnp.exp(pre * pre * (-0.5)) * 0.3989422804014327)
        grad_pre = (grad_hidden * slope).astype(BF)
        hidden_ref[here, :] = hidden
        grad_ref[here, :] = grad_pre
        total += jnp.sum(grad_pre.astype(F32), axis=0, keepdims=True)
        ready.append((hidden, grad_pre))
        if i > 0:
            finish(cuts[i - 1], *ready[i - 1])
    finish(cuts[-1], *ready[-1])
    sums_ref[0:1, :] = total

    @pl.when(step == pl.num_programs(0) - 1)
    def _():
        out_ref[...] = out_sc[...].astype(out_ref.dtype)
        back_ref[...] = back_sc[...].astype(back_ref.dtype)


def ffn(n2, g, w_up, b_up, w_down, dtype):
    rows, width = n2.shape
    units = w_up.shape[1]
    block = 256
    whole = pl.BlockSpec((rows, width), lambda j: (0, 0))
    across = pl.BlockSpec((rows, block), lambda j: (0, j))
    return pl.pallas_call(
        ffn_kernel,
        grid=(units // block,),
        in_specs=[
            whole, whole,
            pl.BlockSpec((width, block), lambda j: (0, j)),
            pl.BlockSpec((1, block), lambda j: (0, j)),
            pl.BlockSpec((block, width), lambda j: (j, 0)),
        ],
        out_specs=[across, across, whole, whole, pl.BlockSpec((8, block), lambda j: (0, j))],
        out_shape=[
            jax.ShapeDtypeStruct((rows, units), BF),
            jax.ShapeDtypeStruct((rows, units), BF),
            jax.ShapeDtypeStruct((rows, width), dtype),
            jax.ShapeDtypeStruct((rows, width), dtype),
            jax.ShapeDtypeStruct((8, units), F32),
        ],
        scratch_shapes=[pltpu.VMEM((rows, width), F32), pltpu.VMEM((rows, width), F32)],
        compiler_params=pltpu.CompilerParams(vmem_limit_bytes=VMEM_LIMIT),
        cost_estimate=pl.CostEstimate(
            flops=8 * rows * width * units, bytes_accessed=int(4 * width * units + 4 * rows * units + 8 * rows * width),
            transcendentals=2 * rows * units,
        ),
        name="ffn",
    )(n2, g, w_up, b_up, w_down)


def norm_back(values, gain, grad):
    center = values - jnp.mean(values, axis=-1, keepdims=True)
    inverse = lax.rsqrt(jnp.mean(center * center, axis=-1, keepdims=True) + EPSILON)
    unit = center * inverse
    scaled = grad * gain
    first = jnp.mean(scaled, axis=-1, keepdims=True)
    second = jnp.mean(scaled * unit, axis=-1, keepdims=True)
    back = (scaled - first - unit * second) * inverse
    return back, jnp.sum(grad * unit, axis=0), jnp.sum(grad, axis=0)


def other_core(a):
    return lax.ppermute(a, "core", [(0, 1), (1, 0)])


def chip_halves(arrays):
    core = lax.axis_index("core")
    halves = [a.reshape(2, a.shape[0] // 2, a.shape[1]) for a in arrays]
    given = [other_core(lax.dynamic_index_in_dim(a, 1 - core, 0, keepdims=False)) for a in halves]
    kept = [lax.dynamic_index_in_dim(a, core, 0, keepdims=False) for a in halves]
    return [(a.astype(F32) + b.astype(F32)).astype(BF) for a, b in zip(kept, given)]


def join_halves(mine):
    first = lax.axis_index("core") == 0
    theirs = [other_core(a) for a in mine]
    return [
        jnp.concatenate([jnp.where(first, a, b), jnp.where(first, b, a)], axis=0) for a, b in zip(mine, theirs)
    ]


def per_device(
    axes, patches, image_of_patch, patch_row, patch_col, ln1_gain, ln1_bias, w_qkv, b_qkv, freqs, w_out, b_out,
    ln2_gain, ln2_bias, w_up, b_up, w_down, b_down, out_cotangent,
):
    own, width = patches.shape
    me = lax.axis_index("mlp")
    other = [(0, 1), (1, 0)]
    swap = lambda a: lax.ppermute(a, "mlp", other)
    edge = min(own, EDGE)
    mine_start = jnp.where(me == 0, own - edge, 0)
    edge_start = jnp.where(me == 0, own, own - edge)
    x_edge = swap(lax.dynamic_slice_in_dim(patches, mine_start, edge))
    g_other = swap(lax.optimization_barrier((out_cotangent, x_edge))[0])

    def local(a):
        return jnp.concatenate(
            [lax.dynamic_slice_in_dim(a[0], me * own, own), lax.dynamic_slice_in_dim(a[0], edge_start, edge)]
        )

    ids = local(image_of_patch)
    row_pos = local(patch_row)[:, None]
    col_pos = local(patch_col)[:, None]
    id_row = ids[None, :]
    id_col = ids[:, None]
    id_own = id_row[:, :own]
    wide_freqs = jnp.concatenate([freqs.reshape(2, H, 1, HD // 2)] * 2, axis=2).reshape(2, width)
    gain1, bias1, bias_qkv = ln1_gain[None], ln1_bias[None], b_qkv[None]
    normed, k_own, v_own, cos_own, sin_own, q, table = input_stage(
        patches, row_pos[:own], col_pos[:own], gain1, bias1, w_qkv, bias_qkv, wide_freqs, True, 256
    )
    normed_edge, k_edge, v_edge, cos_edge, sin_edge = input_stage(
        x_edge, row_pos[own:], col_pos[own:], gain1, bias1, w_qkv, bias_qkv, table, False, edge // 2
    )
    mixed, out_t, lse = attend(id_row, q, k_own, k_edge, v_own, v_edge, id_col, id_own)
    inputs = patches.astype(F32)
    middle = inputs + dot(mixed, w_out) + b_out
    center = middle - jnp.mean(middle, axis=-1, keepdims=True)
    spread = jnp.mean(center * center, axis=-1, keepdims=True)
    normed2 = (center * lax.rsqrt(spread + EPSILON) * ln2_gain + ln2_bias).astype(BF)
    n2_other = swap(normed2)
    bias_up = b_up[None]
    hid_a, gp_a, out_a, back_a, sum_a = ffn(normed2, out_cotangent, w_up, bias_up, w_down, F32)
    hid_b, gp_b, out_b, back_b, sum_b = ffn(n2_other, g_other, w_up, bias_up, w_down, BF)
    back_in = swap(back_b)
    out_in = swap(lax.optimization_barrier((out_b, back_in))[0])
    grad_b_up = sum_a[0] + sum_b[0]
    grad_w_up = (dot_tn(normed2, gp_a) + dot_tn(n2_other, gp_b)).astype(BF)
    grad_w_down = (dot_tn(hid_a, out_cotangent) + dot_tn(hid_b, g_other)).astype(BF)
    ffn_halves = chip_halves([grad_w_up, grad_w_down])
    ffn_halves, back_in = lax.optimization_barrier((ffn_halves, back_in))
    ffn_halves = lax.psum(tuple(ffn_halves), "chip")
    block_out = (middle + out_a + out_in.astype(F32) + b_down).astype(BF)
    grad_out = out_cotangent.astype(F32)
    grad_n2 = back_a + back_in.astype(F32)
    from_norm2, grad_ln2_gain, grad_ln2_bias = norm_back(middle, ln2_gain, grad_n2)
    grad_middle = grad_out + from_norm2
    grad_b_down = jnp.sum(grad_out, axis=0)
    grad_attended = grad_middle.astype(BF)
    grad_b_out = jnp.sum(grad_attended.astype(F32), axis=0)
    grad_w_out = dot_tn(mixed, grad_attended).astype(BF)
    grad_mixed = dot_nt(grad_attended, w_out).astype(BF)
    out_half, grad_mixed = lax.optimization_barrier((chip_halves([grad_w_out])[0], grad_mixed))
    out_half = lax.psum(out_half, ("chip", "mlp"))
    d_own, d_edge, sums = attend_back(
        id_row, q, grad_mixed, k_own, k_edge, v_own, v_edge, id_col, id_own, out_t, lse, row_pos, col_pos,
        (cos_own, sin_own, cos_edge, sin_edge),
    )
    gn_in = swap(dot_nt(d_edge, w_qkv[:, width:]).astype(BF))
    grad_w_q = dot_tn(normed, d_own[:, :width]).astype(BF)
    grad_w_kv = (dot_tn(normed, d_own[:, width:]) + dot_tn(normed_edge, d_edge)).astype(BF)
    gn = dot_nt(d_own, w_qkv)
    spread_in = lax.dynamic_update_slice_in_dim(jnp.zeros((own, width), BF), gn_in, mine_start, 0)
    grad_normed = gn + spread_in.astype(F32)
    from_norm1, grad_ln1_gain, grad_ln1_bias = norm_back(inputs, ln1_gain, grad_normed)
    grad_patches = (grad_middle + from_norm1).astype(BF)
    everyone = axes + ("mlp",)
    units = b_up.shape[0]
    slots = lax.dynamic_update_slice_in_dim(jnp.zeros((2 * units,), F32), grad_b_up, me * units, 0)
    lines = [grad_ln1_gain, grad_ln1_bias, grad_b_out, grad_ln2_gain, grad_ln2_bias, grad_b_down, sums, slots]
    chips = ("chip", "mlp")
    halves = chip_halves([grad_w_q, grad_w_kv])
    halves, lines, out_half = lax.optimization_barrier((halves, lines, out_half))
    halves, lines = lax.optimization_barrier((lax.psum(tuple(halves), chips), lax.psum(tuple(lines), everyone)))
    grad_w_up, grad_w_down = join_halves(ffn_halves)
    grad_w_out = join_halves([out_half])[0]
    grad_w_q, grad_w_kv = join_halves(halves)
    grad_ln1_gain, grad_ln1_bias, grad_b_out, grad_ln2_gain, grad_ln2_bias, grad_b_down, sums, slots = lines
    grad_b_up = lax.dynamic_slice_in_dim(slots, me * units, units)
    grad_w_qkv = jnp.concatenate([grad_w_q, grad_w_kv], axis=1).astype(F32)
    grad_freqs = jnp.sum(sums[3:5].reshape(2, H, 2, HD // 2), axis=2).reshape(2, width // 2)
    return (
        block_out, grad_patches, grad_ln1_gain, grad_ln1_bias, grad_w_qkv, sums[:3].reshape(3 * width), grad_freqs,
        grad_w_out.astype(F32), grad_b_out, grad_ln2_gain, grad_ln2_bias, grad_w_up.astype(F32), grad_b_up,
        grad_w_down.astype(F32), grad_b_down,
    )


def solution(mesh):
    shape = (mesh.shape["dp"] // 2, 2, mesh.shape["mlp"])
    mesh = jax.sharding.Mesh(mesh.devices.reshape(shape), ("chip", "core", "mlp"))
    dp = ("chip", "core")
    rows = P(dp + ("mlp",), None)
    group = P(dp, None)
    in_specs = (rows, group, group, group) + (P(),) * 9 + (P(None, "mlp"), P("mlp"), P("mlp", None), P(), rows)
    out_specs = (rows, rows) + (P(),) * 9 + (P(None, "mlp"), P("mlp"), P("mlp", None), P())
    return jax.shard_map(
        partial(per_device, dp), mesh=mesh, in_specs=in_specs, out_specs=out_specs, check_vma=False
    )
```
